32 devices in a mesh: groups: 2 (over y), gz: 4 (over z), dev: 2 (over x), xy: 2 (over core).
Axes of the slice: x: 2, y: 2, z: 4, core: 2. Of those that a mesh axis runs over, the one named last changes fastest.
Arguments:
- fields: float32 [12, 8, 64, 256], P('groups', 'dev', 'gz', 'xy'), parts along dimension 0, may hold values from -6 to 6
- spectra: float32 [24, 8, 64, 256], P('groups', 'dev', 'gz', 'xy'), parts along dimension 0, may hold values from -6 to 6
- permittivity: float32 [16, 64, 256], P(('groups', 'dev'), 'gz', 'xy'), parts along dimension 0, may hold values from 1 to 12
- phase_start: float32 [2], P('groups'), parts along dimension 0, may hold values from -3.140625 to 3.140625
- wall_owner: int32 [4, 4], P('gz'), may hold values from 0 to 3, as said below
- cap_owner: int32 [2, 32], replicated, may hold values from 0 to 3, as said below
- dir_index: int32 [2048], replicated, may hold values from 0 to 4095
- target: float32 [4096], P('groups'), parts along dimension 0, may hold values from 1 to 12
- aim_mask: int32 [4096], P('groups'), parts along dimension 0, may hold values 0 or 1
Outputs:
- fields_out: float32 [12, 8, 64, 256], P('groups', 'dev', 'gz', 'xy'), parts along dimension 0
- spectra_out: float32 [24, 8, 64, 256], P('groups', 'dev', 'gz', 'xy'), parts along dimension 0
- owned_currents: float32 [8, 2, 2, 20, 128], P(('groups', 'gz'), 'dev', 'xy'), parts along dimension 0
- intensity: float32 [4096], P(('groups', 'gz', 'dev', 'xy')), parts along dimension 0
- adjoint_currents: float32 [8, 2, 2, 36, 128], P(('groups', 'gz'), 'dev', 'xy'), parts along dimension 0
The draws below stay inside these ranges and needn't reach their ends.
There are 2 independent parts, one for each index of `groups`. The reference program is written for one: setup_inputs(seed, part) draws one part's arguments, and reference() takes and returns one part's arrays. A program takes and returns all parts, laid end to end along the dimension named above; an argument that names none is the same for every part. Nothing has to cross between parts.
Inputs may be any that keep to these rules, and one draw needn't show every extreme that they name: `wall_owner`: entry [s, j] names the index of gz that owns wall patch j of slab s; every index owns exactly 4 wall patches of a column, and a slab gives one index at most 1 of them. `cap_owner`: row 0 names the owner on gz of each patch of the lower cap, row 1 of the upper cap; each index owns exactly 8 patches of each cap, so that every index owns exactly 20 patches of a column.
All inputs are finite; a program needn't handle non-finite values.
Results may differ from the reference program's by a relative error of at most 0.0003.
Values sent between devices are 32-bit elements; how exact they have to be, the bound alone decides.
A program may use at most 64 MiB of HBM per device.

```python
import math
import jax
import jax.numpy as jnp
from jax import lax

CX = 128
CY = 4
CZ = 16
PATCH = 16
XB = 8
ZB = 4
STEPS = 3
NDIR = 2048
THETAS = 64
NX = 256
NY = 8
NZ = 64
WALLP = 4
CAPP = 32
OWNED = 20
NSURF = 5120
N_GZ = 4
N_DEV = 2
N_XY = 2


def draw_wall_owner(key, part):
    offsets = jax.random.permutation(jax.random.fold_in(key, 11), N_GZ)
    sources = jnp.arange(N_GZ, dtype=jnp.int32)
    patches = jnp.arange(WALLP, dtype=jnp.int32)
    return ((sources[:, None] + offsets[patches % N_GZ][None, :]) % N_GZ).astype(jnp.int32)


def draw_cap_owner(key, part):
    lower = jax.random.permutation(jax.random.fold_in(key, 21), CAPP) % N_GZ
    upper = jax.random.permutation(jax.random.fold_in(key, 22), CAPP) % N_GZ
    return jnp.stack([lower, upper]).astype(jnp.int32)


def with_ends(entries, stream_key, low, high):
    longest = entries.shape.index(max(entries.shape))
    spots = []
    for shift in (0, 1):
        where = [jax.random.randint(jax.random.fold_in(stream_key, axis), (), 0, length) for axis, length in enumerate(entries.shape)]
        where[longest] = (where[longest] + shift) % entries.shape[longest]
        spots.append(tuple(where))
    return entries.at[spots[0]].set(low).at[spots[1]].set(high)


def levels(own_key, dims, cuts, least, top_value):
    factor_of = 1.0
    for axis_at, shards_of in cuts:
        heights = jax.random.uniform(jax.random.fold_in(jax.random.fold_in(own_key, 6), axis_at), (shards_of,), jnp.float32, least / len(cuts), top_value / len(cuts))
        factor_of = factor_of * jnp.repeat(jnp.exp(heights), dims[axis_at] // shards_of).reshape((-1,) + (1,) * (len(dims) - 1 - axis_at))
    return factor_of


def gaussian(stream_key, shape, deviation, limit, shards=(), held_as=jnp.bfloat16):
    drawn = deviation * jax.random.normal(stream_key, shape, jnp.float32)
    if shards:
        drawn = drawn * levels(stream_key, shape, shards, -0.22, 0.18)
    return jnp.clip(drawn, -limit, limit).astype(held_as)


def setup_inputs(seed: int = 0, part: int = 0) -> dict:
    streams_of = jax.random.split(jax.random.key(seed), 10)
    own_keys = jax.random.split(jax.random.fold_in(streams_of[9], part), 10)
    return {
        "fields": gaussian(own_keys[0], (6, NY, NZ, NX), 1.0, 6.0, ((1, 2), (2, 4), (3, 2)), jnp.float32),
        "spectra": gaussian(own_keys[1], (12, NY, NZ, NX), 1.0, 6.0, ((1, 2), (2, 4), (3, 2)), jnp.float32),
        "permittivity": jnp.clip(jnp.exp(math.log(12.0) - 2.4849066 * jax.random.uniform(own_keys[2], (NY, NZ, NX), jnp.float32) ** levels(own_keys[2], (NY, NZ, NX), ((0, 2), (1, 4), (2, 2)), -0.2, 0.2)), 1.0, 12.0),
        "phase_start": jnp.clip(jax.random.uniform(own_keys[3], (1,), jnp.float32, -3.140625, 3.140625), -3.140625, 3.140625),
        "wall_owner": draw_wall_owner(jax.random.fold_in(streams_of[9], 71), part),
        "cap_owner": draw_cap_owner(jax.random.fold_in(streams_of[9], 71), part),
        "dir_index": with_ends(jax.random.randint(streams_of[6], (NDIR,), 0, THETAS * THETAS), jax.random.fold_in(streams_of[6], 1), 0, (THETAS * THETAS) - 1).astype(jnp.int32),
        "target": jnp.clip(jax.random.uniform(own_keys[7], (NDIR,), jnp.float32, 1.0, 12.0), 1.0, 12.0),
        "aim_mask": with_ends((jax.random.randint(own_keys[8], (NDIR,), 0, 4) < 3).astype(jnp.int32), jax.random.fold_in(own_keys[8], 1), 0, 1),
    }


COURANT = 0.5
ANGULAR_STEP = 0.3
WAVE_NUMBER = 0.6
HIGHEST = lax.Precision.HIGHEST
CURRENT_SIGNS = (-1.0, 1.0, 1.0, -1.0)
X_PICKS = (5, 4, 2, 1)
Z_PICKS = (4, 3, 1, 0)

def ahead_diff(values, axis_number):
    length = values.shape[axis_number]
    shifted = jnp.concatenate([lax.slice_in_dim(values, 1, length, axis=axis_number), jnp.zeros_like(lax.slice_in_dim(values, 0, 1, axis=axis_number))], axis=axis_number)
    return shifted - values

def behind_diff(values, axis_number):
    length = values.shape[axis_number]
    shifted = jnp.concatenate([jnp.zeros_like(lax.slice_in_dim(values, 0, 1, axis=axis_number)), lax.slice_in_dim(values, 0, length - 1, axis=axis_number)], axis=axis_number)
    return values - shifted

def spectral_update(spectra_now, electric, magnetic, phase_start, step_number):
    angle_half = phase_start[0] + ANGULAR_STEP * (step_number + 0.5)
    angle_full = phase_start[0] + ANGULAR_STEP * (step_number + 1.0)
    return jnp.concatenate([spectra_now[0:3] + electric * jnp.cos(angle_full), spectra_now[3:6] + magnetic * jnp.cos(angle_half), spectra_now[6:9] - electric * jnp.sin(angle_full), spectra_now[9:12] - magnetic * jnp.sin(angle_half)])

def face_values(spectral_plane, facing, chosen):
    real_part = [CURRENT_SIGNS[number] * facing * spectral_plane[chosen[number]] for number in range(4)]
    imag_part = [CURRENT_SIGNS[number] * facing * spectral_plane[6 + chosen[number]] for number in range(4)]
    return jnp.stack(real_part + imag_part)

def to_vectors(record_values, x_flag):
    z_flag = 1.0 - x_flag
    stacked_rows = []
    for offset in (0, 4):
        tangent_one = record_values[offset]
        tangent_two = record_values[offset + 1]
        moment_one = record_values[offset + 2]
        moment_two = record_values[offset + 3]
        stacked_rows += [z_flag * tangent_one, x_flag * tangent_one + z_flag * tangent_two, x_flag * tangent_two, z_flag * moment_one, x_flag * moment_one + z_flag * moment_two, x_flag * moment_two]
    return jnp.stack(stacked_rows)

def to_record(gradient, x_flag):
    z_flag = 1.0 - x_flag
    stacked_rows = []
    for offset in (0, 6):
        stacked_rows += [x_flag * gradient[offset + 1] + z_flag * gradient[offset], x_flag * gradient[offset + 2] + z_flag * gradient[offset + 1], x_flag * gradient[offset + 4] + z_flag * gradient[offset + 3], x_flag * gradient[offset + 5] + z_flag * gradient[offset + 4]]
    return jnp.stack(stacked_rows)

def direction_frames(dir_index):
    polar_row = (dir_index // THETAS).astype(jnp.float32)
    azimuth_col = (dir_index % THETAS).astype(jnp.float32)
    polar_angle = jnp.pi * (polar_row + 0.5) / THETAS
    azimuth = 2.0 * jnp.pi * azimuth_col / THETAS
    sin_polar = jnp.sin(polar_angle)
    cos_polar = jnp.cos(polar_angle)
    sin_azim = jnp.sin(azimuth)
    cos_azim = jnp.cos(azimuth)
    unit_vectors = jnp.stack([sin_polar * cos_azim, sin_polar * sin_azim, cos_polar], axis=1)
    theta_hat = jnp.stack([cos_polar * cos_azim, cos_polar * sin_azim, -sin_polar], axis=1)
    phi_hat = jnp.stack([-sin_azim, cos_azim, jnp.zeros_like(sin_azim)], axis=1)
    return (unit_vectors, theta_hat, phi_hat)

def steering(unit_block, positions):
    angle_table = WAVE_NUMBER * (positions[0][:, None] * unit_block[None, :, 0] + positions[1][:, None] * unit_block[None, :, 1] + positions[2][:, None] * unit_block[None, :, 2])
    return (jnp.cos(angle_table), jnp.sin(angle_table))

def far_block(unit_block, currents, positions):
    cosine_table, sine_table = steering(unit_block, positions)
    real_part = jnp.dot(currents[:6], cosine_table, precision=HIGHEST) - jnp.dot(currents[6:], sine_table, precision=HIGHEST)
    imag_part = jnp.dot(currents[:6], sine_table, precision=HIGHEST) + jnp.dot(currents[6:], cosine_table, precision=HIGHEST)
    return jnp.concatenate([real_part, imag_part], axis=0)

def adjoint_block(unit_block, slope_block, positions):
    cosine_table, sine_table = steering(unit_block, positions)
    real_part = jnp.dot(slope_block[:6], cosine_table.T, precision=HIGHEST) + jnp.dot(slope_block[6:], sine_table.T, precision=HIGHEST)
    imag_part = jnp.dot(slope_block[6:], cosine_table.T, precision=HIGHEST) - jnp.dot(slope_block[:6], sine_table.T, precision=HIGHEST)
    return jnp.concatenate([real_part, imag_part], axis=0)

def intensity_and_slope(far_total, theta_hat, phi_hat, target, aim_mask):
    theta_rows = theta_hat.T
    phi_rows = phi_hat.T

    def project(vectors, frame_rows):
        return lax.optimization_barrier(jnp.sum(vectors * frame_rows, axis=0))
    e_theta_re = -(project(far_total[3:6], phi_rows) + project(far_total[0:3], theta_rows))
    e_phi_re = project(far_total[3:6], theta_rows) - project(far_total[0:3], phi_rows)
    e_theta_im = -(project(far_total[9:12], phi_rows) + project(far_total[6:9], theta_rows))
    e_phi_im = project(far_total[9:12], theta_rows) - project(far_total[6:9], phi_rows)
    intensity = e_theta_re * e_theta_re + e_theta_im * e_theta_im + e_phi_re * e_phi_re + e_phi_im * e_phi_im
    residual = aim_mask.astype(jnp.float32) * (intensity - target)
    slope_theta_re = 2.0 * residual * e_theta_re
    slope_phi_re = 2.0 * residual * e_phi_re
    slope_theta_im = 2.0 * residual * e_theta_im
    slope_phi_im = 2.0 * residual * e_phi_im
    n_re = -slope_theta_re * theta_rows - slope_phi_re * phi_rows
    l_re = -slope_theta_re * phi_rows + slope_phi_re * theta_rows
    n_im = -slope_theta_im * theta_rows - slope_phi_im * phi_rows
    l_im = -slope_theta_im * phi_rows + slope_phi_im * theta_rows
    return (intensity, jnp.concatenate([n_re, l_re, n_im, l_im], axis=0))

def arrange(wall_values, cap_values):
    walls = wall_values.reshape(N_XY, 8, N_DEV, CY, N_GZ, CZ).transpose(4, 2, 0, 1, 3, 5)
    walls = walls.reshape(N_GZ, N_DEV, N_XY, 8, WALLP, PATCH).transpose(0, 1, 2, 4, 3, 5).reshape(N_GZ, N_DEV, N_XY, WALLP, 8 * PATCH)
    caps = cap_values.reshape(2, 8, N_DEV, CY, N_XY, CX).transpose(0, 2, 4, 1, 3, 5)
    caps = caps.reshape(2, N_DEV, N_XY, 8, CAPP, PATCH).transpose(0, 1, 2, 4, 3, 5).reshape(2, N_DEV, N_XY, CAPP, 8 * PATCH)
    middle = jnp.zeros((N_GZ - 2, N_DEV, N_XY, CAPP, 8 * PATCH), jnp.float32)
    cap_rows = jnp.concatenate([caps[0:1], middle, caps[1:2]], axis=0)
    return jnp.concatenate([walls, cap_rows], axis=3)

def gather_owned(records, wall_owner, cap_owner):
    flat_walls = records[:, :, :, :WALLP].transpose(0, 3, 1, 2, 4).reshape(N_GZ * WALLP, N_DEV, N_XY, 8 * PATCH)
    caps_lower = records[0, :, :, WALLP:].transpose(2, 0, 1, 3)
    caps_upper = records[N_GZ - 1, :, :, WALLP:].transpose(2, 0, 1, 3)
    flat_records = jnp.concatenate([flat_walls, caps_lower, caps_upper], axis=0)
    owner_flat = jnp.concatenate([wall_owner.reshape(N_GZ * WALLP), cap_owner[0], cap_owner[1]]).astype(jnp.int32)
    total = N_GZ * WALLP + 2 * CAPP
    flat_order = jnp.arange(total, dtype=jnp.int32)
    earlier_same = (owner_flat[:, None] == owner_flat[None, :]) & (flat_order[None, :] < flat_order[:, None])
    slot_rank = lax.optimization_barrier(jnp.sum(earlier_same.astype(jnp.int32), axis=1)).astype(jnp.int32)
    owner_range = jnp.arange(N_GZ, dtype=jnp.int32)
    place_range = jnp.arange(OWNED, dtype=jnp.int32)
    matches = (owner_flat[None, None, :] == owner_range[:, None, None]) & (slot_rank[None, None, :] == place_range[None, :, None])
    selector = jnp.where(matches, 1.0, 0.0).astype(jnp.float32)
    return jnp.einsum('okg,gdhr->odhkr', selector, flat_records, precision=HIGHEST)

def reference(fields, spectra, permittivity, phase_start, wall_owner, cap_owner, dir_index, target, aim_mask):
    step_rate = COURANT / permittivity
    electric_list = [fields[0], fields[1], fields[2]]
    magnetic_list = [fields[3], fields[4], fields[5]]
    spectra_now = spectra
    for step_number in range(STEPS):
        magn_x = magnetic_list[0] - COURANT * (ahead_diff(electric_list[2], 0) - ahead_diff(electric_list[1], 1))
        magn_y = magnetic_list[1] - COURANT * (ahead_diff(electric_list[0], 1) - ahead_diff(electric_list[2], 2))
        magn_z = magnetic_list[2] - COURANT * (ahead_diff(electric_list[1], 2) - ahead_diff(electric_list[0], 0))
        magnetic_list = [magn_x, magn_y, magn_z]
        elec_x = electric_list[0] + step_rate * (behind_diff(magn_z, 0) - behind_diff(magn_y, 1))
        elec_y = electric_list[1] + step_rate * (behind_diff(magn_x, 1) - behind_diff(magn_z, 2))
        elec_z = electric_list[2] + step_rate * (behind_diff(magn_y, 2) - behind_diff(magn_x, 0))
        electric_list = [elec_x, elec_y, elec_z]
        spectra_now = spectral_update(spectra_now, jnp.stack(electric_list), jnp.stack(magnetic_list), phase_start, step_number)
    fields_out = jnp.stack(electric_list + magnetic_list)
    wall_values = jnp.stack([face_values(spectra_now[:, :, :, XB], -1.0, X_PICKS), face_values(spectra_now[:, :, :, NX - 1 - XB], 1.0, X_PICKS)])
    cap_values = jnp.stack([face_values(spectra_now[:, :, ZB, :], -1.0, Z_PICKS), face_values(spectra_now[:, :, NZ - 1 - ZB, :], 1.0, Z_PICKS)])
    records = arrange(wall_values, cap_values)
    owned_currents = gather_owned(records, wall_owner, cap_owner)
    wall_points = 2 * NY * NZ
    cap_points = 2 * NY * NX
    point_values = jnp.concatenate([wall_values.transpose(1, 0, 2, 3).reshape(8, wall_points), cap_values.transpose(1, 0, 2, 3).reshape(8, cap_points)], axis=1)
    x_flag = jnp.concatenate([jnp.ones((wall_points,), jnp.float32), jnp.zeros((cap_points,), jnp.float32)])
    y_grid = jnp.arange(NY, dtype=jnp.float32) - (NY - 1) / 2.0
    z_grid = jnp.arange(NZ, dtype=jnp.float32) - (NZ - 1) / 2.0
    x_grid = jnp.arange(NX, dtype=jnp.float32) - (NX - 1) / 2.0
    wall_x = jnp.array([XB, NX - 1 - XB], dtype=jnp.float32) - (NX - 1) / 2.0
    cap_z = jnp.array([ZB, NZ - 1 - ZB], dtype=jnp.float32) - (NZ - 1) / 2.0
    wall_shape = (2, NY, NZ)
    cap_shape = (2, NY, NX)
    wall_positions = jnp.stack([jnp.broadcast_to(wall_x[:, None, None], wall_shape), jnp.broadcast_to(y_grid[None, :, None], wall_shape), jnp.broadcast_to(z_grid[None, None, :], wall_shape)]).reshape(3, wall_points)
    cap_positions = jnp.stack([jnp.broadcast_to(x_grid[None, None, :], cap_shape), jnp.broadcast_to(y_grid[None, :, None], cap_shape), jnp.broadcast_to(cap_z[:, None, None], cap_shape)]).reshape(3, cap_points)
    positions = jnp.concatenate([wall_positions, cap_positions], axis=1)
    norm_scale = 1.0 / math.sqrt(2.0 * NSURF)
    currents = to_vectors(point_values, x_flag) * norm_scale
    unit_vectors, theta_hat, phi_hat = direction_frames(dir_index)
    block_rows = 128
    unit_blocks = unit_vectors.reshape(NDIR // block_rows, block_rows, 3)

    def far_of_block(unit_block):
        return far_block(unit_block, currents, positions)
    far_total = lax.map(far_of_block, unit_blocks).transpose(1, 0, 2).reshape(12, NDIR)
    intensity, slope_total = intensity_and_slope(far_total, theta_hat, phi_hat, target, aim_mask)
    slope_blocks = slope_total.reshape(12, NDIR // block_rows, block_rows).transpose(1, 0, 2)

    def add_block(carry_sum, pieces):
        return (carry_sum + adjoint_block(pieces[0], pieces[1], positions), None)
    gradient, ignored = lax.scan(add_block, jnp.zeros((12, NSURF), jnp.float32), (unit_blocks, slope_blocks))
    point_adjoint = to_record(gradient * norm_scale, x_flag)
    adjoint_walls = point_adjoint[:, :wall_points].reshape(8, 2, NY, NZ).transpose(1, 0, 2, 3)
    adjoint_caps = point_adjoint[:, wall_points:].reshape(8, 2, NY, NX).transpose(1, 0, 2, 3)
    adjoint_currents = arrange(adjoint_walls, adjoint_caps)
    return (fields_out, spectra_now, owned_currents, intensity, adjoint_currents)
```

```python
import functools
import math

import jax
import jax.numpy as jnp
from jax import lax
from jax.experimental import pallas as pl
from jax.experimental.pallas import tpu as pltpu
from jax.sharding import PartitionSpec as P

PATCH = 16
XB = 8
ZB = 4
STEPS = 3
THETAS = 64
COURANT = 0.5
ANGULAR_STEP = 0.3
WAVE_NUMBER = 0.6
LANES = 128
HIGHEST = lax.Precision.HIGHEST
CURRENT_SIGNS = (-1.0, 1.0, 1.0, -1.0)
X_PICKS = (5, 4, 2, 1)
Z_PICKS = (4, 3, 1, 0)
MESH = pl.DeviceIdType.MESH
AXES = ("dev", "gz", "xy")
F32 = jnp.float32
BF16 = jnp.bfloat16


def iota(shape, dim):
    return lax.broadcasted_iota(jnp.int32, shape, dim)


def sincos(turns):
    half = (turns - jnp.floor(turns + 0.5)) * math.pi
    sq = half * half
    sin_h = half * (1.0 + sq * (-1.0 / 6 + sq * (1.0 / 120 + sq * (-1.0 / 5040 + sq * (1.0 / 362880 - sq * (1.0 / 39916800))))))
    cos_h = 1.0 + sq * (-0.5 + sq * (1.0 / 24 + sq * (-1.0 / 720 + sq * (1.0 / 40320 + sq * (-1.0 / 3628800 + sq * (1.0 / 479001600))))))
    return 2.0 * sin_h * cos_h, 1.0 - 2.0 * sin_h * sin_h


def split(values):
    high = values.astype(BF16)
    return high, (values - high.astype(F32)).astype(BF16)


def block_transpose(tile):
    on_diagonal = (iota(tile.shape, 1) // PATCH) == iota(tile.shape, 0)
    total = jnp.where(on_diagonal, tile, 0.0)
    for k in range(1, 8):
        turned = pltpu.roll(tile, PATCH * k, 1)
        total = total + pltpu.roll(jnp.where(on_diagonal, turned, 0.0), 8 - k, 0)
    return total


def kernel(
    sizes,
    fields, spectra, permit, phase, wall_owner, cap_owner, dirs, target, aim,
    fields_out, spectra_out, owned_out, intensity_out, adjoint_out,
    send_y, send_z, send_x, got_y, got_z, got_x,
    geo, weights, phases, table_hi, table_lo, cap_plane, lhs,
    parts_out, parts_in, slopes, walls, caps,
    halo_send, halo_got, part_send, part_got, slope_send, slope_got, wall_send, wall_got, cap_send, cap_got,
):
    slabs, devs, xys = sizes
    peers = slabs * devs * xys
    size_y, size_z, size_x = permit.shape
    chunks = dirs.shape[0]
    ratio = peers // chunks
    groups = 2 * size_y
    half_rows = 8 * size_y
    all_rows = 2 * half_rows
    gz, dev, xy = lax.axis_index("gz"), lax.axis_index("dev"), lax.axis_index("xy")
    me = (gz * devs + dev) * xys + xy
    place = {"dev": dev, "gz": gz, "xy": xy}
    count = {"dev": devs, "gz": slabs, "xy": xys}

    def ident(flat):
        return {"gz": flat // (devs * xys), "dev": (flat // xys) % devs, "xy": flat % xys}

    barrier = pltpu.get_barrier_semaphore()

    def greet(k, carry):
        pl.semaphore_signal(barrier, inc=1, device_id=ident((me + k) % peers), device_id_type=MESH)
        return carry

    lax.fori_loop(1, peers, greet, 0)

    index = dirs[...]
    sin_t, cos_t = sincos(((index // THETAS).astype(F32) + 0.5) * (0.5 / THETAS))
    sin_f, cos_f = sincos((index % THETAS).astype(F32) * (1.0 / THETAS))
    wave = WAVE_NUMBER / (2.0 * math.pi)
    for slot, values in enumerate((
        wave * sin_t * cos_f, wave * sin_t * sin_f, wave * cos_t,
        cos_t * cos_f, cos_t * sin_f, -sin_t, -sin_f, cos_f,
    )):
        geo[slot] = values

    grid_x, grid_y, grid_z = size_x * xys, size_y * devs, size_z * slabs
    x_first = (xy * size_x).astype(F32) - (grid_x - 1) / 2.0
    y_first = (dev * size_y).astype(F32) - (grid_y - 1) / 2.0
    z_first = (gz * size_z).astype(F32) - (grid_z - 1) / 2.0
    x_wall = jnp.where(xy == 0, XB, size_x - 1 - XB)
    z_cap = jnp.where(gz == 0, ZB, size_z - 1 - ZB)
    x_face = x_first + x_wall.astype(F32)
    z_face = z_first + z_cap.astype(F32)
    facing_x = jnp.where(xy == 0, -1.0, 1.0)
    facing_z = jnp.where(gz == 0, -1.0, 1.0)
    is_end = jnp.logical_or(gz == 0, gz == slabs - 1)
    end_weight = jnp.where(is_end, 1.0, 0.0)
    norm = 1.0 / math.sqrt(2.0 * (2 * grid_y * grid_z + 2 * grid_y * grid_x))

    def make_tables(j, carry):
        def row(slot):
            return geo[slot, pl.ds(j, 1), :]

        ux, uy, uz = row(0), row(1), row(2)
        blocks = size_x // 8
        far_s, far_c = sincos((iota((blocks, LANES), 0).astype(F32) * 8.0 + x_first) * ux)
        near_s, near_c = sincos(iota((8, LANES), 0).astype(F32) * ux)
        far_s, far_c = far_s[:, None, :], far_c[:, None, :]
        near_s, near_c = near_s[None], near_c[None]
        cos_x = (far_c * near_c - far_s * near_s).reshape(size_x, LANES)
        sin_x = (far_s * near_c + far_c * near_s).reshape(size_x, LANES)
        sin_z, cos_z = sincos((iota((size_z, LANES), 0).astype(F32) + z_first) * uz)
        for at, (x_part, z_part) in enumerate(((cos_x, cos_z), (sin_x, sin_z))):
            lanes = pl.ds(at * LANES, LANES)
            x_high, x_low = split(x_part)
            z_high, z_low = split(z_part)
            table_hi[j, pl.ds(0, size_x), lanes] = x_high
            table_lo[j, pl.ds(0, size_x), lanes] = x_low
            table_hi[j, pl.ds(size_x, 8 * size_z), lanes] = jnp.concatenate([z_high] * 8, axis=0)
            table_lo[j, pl.ds(size_x, 8 * size_z), lanes] = jnp.concatenate([z_low] * 8, axis=0)
        which = iota((groups, LANES), 0)
        cell_y = (which % size_y).astype(F32) + y_first
        sin_g, cos_g = sincos(cell_y * uy + jnp.where(which < size_y, z_face * uz, x_face * ux))
        phases[j, 0] = cos_g
        phases[j, 1] = sin_g
        kind = iota((8, LANES), 0) % 4

        def pattern(a, b, c, d):
            return jnp.where(kind == 0, a, jnp.where(kind == 1, b, jnp.where(kind == 2, c, d)))

        tx, ty, tz, fx, fy = row(3), row(4), row(5), row(6), row(7)
        weights[j, 0] = pattern(-tx, -ty, -fx, -fy)
        weights[j, 1] = pattern(-fx, -fy, tx, ty)
        weights[j, 2] = pattern(-ty, -tz, -fy, jnp.zeros_like(fy))
        weights[j, 3] = pattern(-fy, jnp.zeros_like(fy), ty, tz)
        return carry

    windows = 2 * STEPS

    def tables_of(window):
        lax.fori_loop(window * chunks // windows, (window + 1) * chunks // windows, make_tables, 0)

    order = iota((8, LANES), 0).astype(F32)
    run_s, run_c = sincos((phase[0] + 0.5 * ANGULAR_STEP * (order + 1.0)) * (0.5 / math.pi))

    for number, (axis, got) in enumerate(zip(AXES, (got_y, got_z, got_x))):
        @pl.when(place[axis] == count[axis] - 1)
        def _():
            for window in range(0, windows, 2):
                got[window] = jnp.zeros(got.shape[1:], F32)

        @pl.when(place[axis] == 0)
        def _():
            for window in range(1, windows, 2):
                got[window] = jnp.zeros(got.shape[1:], F32)

    pl.semaphore_wait(barrier, peers - 1)

    lane = iota((size_z, LANES), 1)
    lane3 = iota((size_y, size_z, LANES), 2)
    row3 = iota((size_y, size_z, LANES), 1)

    def halo_copies(window):
        step = -1 if window % 2 == 0 else 1
        copies = []
        for number, (axis, source, landing) in enumerate(
            zip(AXES, (send_y, send_z, send_x), (got_y, got_z, got_x))
        ):
            mine, total = place[axis], count[axis]
            copy = pltpu.make_async_remote_copy(
                src_ref=source.at[window],
                dst_ref=landing.at[window],
                send_sem=halo_send.at[window, number],
                recv_sem=halo_got.at[window, number],
                device_id={axis: (mine + step + total) % total},
                device_id_type=MESH,
            )
            if step < 0:
                copies.append((copy, mine > 0, mine < total - 1))
            else:
                copies.append((copy, mine < total - 1, mine > 0))
        return copies

    def start_halo(window, for_y, for_z, for_x):
        ahead = window % 2 == 0
        at_y, at_z = (0, 0) if ahead else (size_y - 1, size_z - 1)
        for k in range(2):
            send_y[window, k] = for_y[k][at_y]
            send_z[window, k] = for_z[k][:, at_z : at_z + 1, :]
        packed = jnp.zeros((size_z, LANES), F32)
        for k in range(2):
            for y in range(size_y):
                spot = k * size_y + y
                amount = spot if ahead else (spot + 1) % LANES
                value = for_x[k][y]
                turned = pltpu.roll(value, amount, 1) if amount else value
                packed = jnp.where(lane == spot, turned, packed)
        send_x[window] = packed
        for copy, sends, receives in halo_copies(window):
            @pl.when(sends)
            def _():
                copy.start()

    def wait_halo(window):
        for copy, sends, receives in halo_copies(window):
            @pl.when(receives)
            def _():
                copy.wait_recv()

    def shift_y(window, k, value):
        other = got_y[window, k][None]
        if window % 2 == 0:
            return jnp.concatenate([value[1:], other], axis=0) - value
        return value - jnp.concatenate([other, value[:-1]], axis=0)

    def shift_z(window, k, value):
        other = got_z[window, k]
        if window % 2 == 0:
            return jnp.where(row3 == size_z - 1, other, pltpu.roll(value, size_z - 1, 1)) - value
        return value - jnp.where(row3 == 0, other, pltpu.roll(value, 1, 1))

    def shift_x(window, k, value):
        landed = got_x[window]
        edges = []
        for y in range(size_y):
            spot = k * size_y + y
            if window % 2 == 0:
                edges.append(pltpu.roll(landed, LANES - 1 - spot, 1))
            else:
                amount = (LANES - spot) % LANES
                edges.append(pltpu.roll(landed, amount, 1) if amount else landed)
        other = jnp.stack(edges, axis=0)
        if window % 2 == 0:
            return jnp.where(lane3 == size_x - 1, other, pltpu.roll(value, size_x - 1, 2)) - value
        return value - jnp.where(lane3 == 0, other, pltpu.roll(value, 1, 2))

    ex, ey, ez = fields[0], fields[1], fields[2]
    start_halo(0, (ez, ex), (ey, ex), (ez, ey))
    rate = COURANT / permit[...]
    hx, hy, hz = fields[3], fields[4], fields[5]
    spec_from = spectra
    for n in range(STEPS):
        window = 2 * n
        tables_of(window)
        wait_halo(window)
        hx = hx - COURANT * (shift_y(window, 0, ez) - shift_z(window, 0, ey))
        hy = hy - COURANT * (shift_z(window, 1, ex) - shift_x(window, 0, ez))
        hz = hz - COURANT * (shift_x(window, 1, ey) - shift_y(window, 1, ex))
        window = 2 * n + 1
        start_halo(window, (hz, hx), (hy, hx), (hz, hy))
        half_c, half_s = run_c[2 * n : 2 * n + 1, :], run_s[2 * n : 2 * n + 1, :]
        for c, value in enumerate((hx, hy, hz)):
            spectra_out[3 + c] = spec_from[3 + c] + value * half_c
            spectra_out[9 + c] = spec_from[9 + c] - value * half_s
        tables_of(window)
        wait_halo(window)
        ex = ex + rate * (shift_y(window, 0, hz) - shift_z(window, 0, hy))
        ey = ey + rate * (shift_z(window, 1, hx) - shift_x(window, 0, hz))
        ez = ez + rate * (shift_x(window, 1, hy) - shift_y(window, 1, hx))
        if n < STEPS - 1:
            start_halo(window + 1, (ez, ex), (ey, ex), (ez, ey))
        full_c, full_s = run_c[2 * n + 1 : 2 * n + 2, :], run_s[2 * n + 1 : 2 * n + 2, :]
        for c, value in enumerate((ex, ey, ez)):
            spectra_out[c] = spec_from[c] + value * full_c
            spectra_out[6 + c] = spec_from[6 + c] - value * full_s
        spec_from = spectra_out
    for c, value in enumerate((ex, ey, ez, hx, hy, hz)):
        fields_out[c] = value

    own_walls = walls.at[gz]
    lane_block = iota((8, LANES), 1) // PATCH
    sub = iota((8, LANES), 0)
    own_block = lane_block == sub
    z_row = iota((size_z, LANES), 0)
    own_walls[...] = jnp.zeros((8, LANES), F32)
    for y in range(size_y):
        spread = jnp.zeros((size_z, LANES), F32)
        for c in range(8):
            k = c % 4
            from_c = X_PICKS[k] + (6 if c >= 4 else 0)
            column = jnp.sum(jnp.where(lane == x_wall, spectra_out[from_c, y], 0.0), axis=1, keepdims=True)
            spread = jnp.where(lane == c * PATCH + z_row, column * (CURRENT_SIGNS[k] * facing_x), spread)
        record = jnp.sum(spread, axis=0, keepdims=True)
        own_walls[pl.ds(y, 1), :] = record
        for c in range(8):
            k = c % 4
            from_c = Z_PICKS[k] + (6 if c >= 4 else 0)
            low = spectra_out[from_c, y, pl.ds(ZB, 1), :]
            high = spectra_out[from_c, y, pl.ds(size_z - 1 - ZB, 1), :]
            picked = jnp.where(gz == 0, low, high) * (CURRENT_SIGNS[k] * facing_z * end_weight)
            cap_plane[pl.ds(8 * y + c, 1), :] = picked
        wall_hi, wall_lo = split(jnp.where(own_block, record, 0.0) * norm)
        cap_hi, cap_lo = split(cap_plane[pl.ds(8 * y, 8), :] * norm)
        none = jnp.zeros((8, LANES), BF16)
        for at, (cap_part, wall_part) in enumerate(((cap_hi, wall_hi), (cap_lo, wall_lo))):
            first = at * all_rows + 8 * y
            lhs[pl.ds(first, 8), :] = jnp.concatenate([cap_part, none], axis=1)
            lhs[pl.ds(first + half_rows, 8), :] = jnp.concatenate([none, wall_part], axis=1)

    sign = jnp.where(sub < 4, -1.0, 1.0)

    def far_of(j, carry):
        rows = lhs[...]
        by_high = jnp.dot(rows, table_hi[j], preferred_element_type=F32)
        by_low = jnp.dot(rows[:all_rows], table_lo[j], preferred_element_type=F32)
        product = by_high[:all_rows] + by_high[all_rows:] + by_low
        theta = jnp.zeros((8, LANES), F32)
        phi = jnp.zeros((8, LANES), F32)
        for face in range(2):
            sum_c = jnp.zeros((8, LANES), F32)
            sum_s = jnp.zeros((8, LANES), F32)
            for y in range(size_y):
                g = face * size_y + y
                tile = product[8 * g : 8 * g + 8]
                tile = tile[:, :LANES] + sign * pltpu.roll(tile[:, LANES:], 4, 0)
                sum_c = sum_c + tile * phases[j, 0, pl.ds(g, 1), :]
                sum_s = sum_s + tile * phases[j, 1, pl.ds(g, 1), :]
            far = sum_c + sign * pltpu.roll(sum_s, 4, 0)
            theta = theta + weights[j, 2 * face] * far
            phi = phi + weights[j, 2 * face + 1] * far

        def four(values):
            pairs = values + pltpu.roll(values, 7, 0)
            return pairs + pltpu.roll(pairs, 6, 0)

        parts_out[j] = jnp.where(sub % 4 == 1, pltpu.roll(four(phi), 1, 0), four(theta))
        return carry

    lax.fori_loop(0, chunks, far_of, 0)

    def part_copy(k):
        peer = (me + k) % peers
        return pltpu.make_async_remote_copy(
            src_ref=parts_out.at[peer // ratio],
            dst_ref=parts_in.at[k],
            send_sem=part_send.at[k],
            recv_sem=part_got.at[k],
            device_id=ident(peer),
            device_id_type=MESH,
        )

    def each_peer(act):
        def body(k, carry):
            act(k)
            return carry

        lax.fori_loop(1, peers, body, 0)

    each_peer(lambda k: part_copy(k).start())

    lanes8 = iota((1, LANES), 1)
    owner_row = jnp.zeros((1, LANES), F32)
    for p in range(size_y):
        owner_row = jnp.where(lanes8 == 8 * gz + p, (wall_owner[0, p] + 1).astype(F32), owner_row)
    own_walls[pl.ds(size_y, 1), :] = owner_row

    def wall_copy(k):
        return pltpu.make_async_remote_copy(
            src_ref=walls.at[gz],
            dst_ref=walls.at[gz],
            send_sem=wall_send.at[k],
            recv_sem=wall_got.at[gz],
            device_id={"gz": (gz + k) % slabs},
            device_id_type=MESH,
        )

    def wall_landing(s):
        return pltpu.make_async_remote_copy(
            src_ref=walls.at[s], dst_ref=walls.at[s], send_sem=wall_send.at[0], recv_sem=wall_got.at[s],
            device_id={"gz": (gz + 1) % slabs}, device_id_type=MESH,
        )

    def cap_copy(k, at):
        return pltpu.make_async_remote_copy(
            src_ref=caps.at[at],
            dst_ref=caps.at[at],
            send_sem=cap_send.at[k],
            recv_sem=cap_got.at[at],
            device_id={"gz": (gz + k) % slabs},
            device_id_type=MESH,
        )

    for k in range(1, slabs):
        wall_copy(k).start()
    for at, holder in enumerate((0, slabs - 1)):
        @pl.when(gz == holder)
        def _():
            for y in range(size_y):
                caps[at, pl.ds(8 * y, 8), :] = block_transpose(cap_plane[pl.ds(8 * y, 8), :])
            for k in range(1, slabs):
                cap_copy(k, at).start()

    parts_in[0] = parts_out[me // ratio]
    each_peer(lambda k: part_copy(k).wait_recv())
    field = jnp.sum(parts_in[...], axis=0)
    chunk = me // ratio
    power = jnp.where(sub % 4 < 2, field * field, 0.0)
    intensity = jnp.sum(power, axis=0, keepdims=True)
    intensity_out[...] = intensity
    residual = aim[pl.ds(chunk, 1), :].astype(F32) * (intensity - target[pl.ds(chunk, 1), :])
    leads = me % ratio == 0

    def slope_copy(k, of):
        return pltpu.make_async_remote_copy(
            src_ref=slopes.at[of],
            dst_ref=slopes.at[of],
            send_sem=slope_send.at[k],
            recv_sem=slope_got.at[of],
            device_id=ident((me + k) % peers),
            device_id_type=MESH,
        )

    @pl.when(leads)
    def _():
        slopes[chunk] = 2.0 * residual * field
        each_peer(lambda k: slope_copy(k, chunk).start())

    for s in range(slabs):
        @pl.when(s != gz)
        def _():
            wall_landing(s).wait_recv()
    for at, holder in enumerate((0, slabs - 1)):
        @pl.when(gz != holder)
        def _():
            cap_copy(1, at).wait_recv()

    def choose(mine, share, records):
        length = mine.shape[1]
        before = jnp.where(iota((length, length), 0) < iota((length, length), 1), 1.0, 0.0).astype(BF16)
        ones = jnp.broadcast_to(jnp.where(mine, 1.0, 0.0), (8, length))
        rank = jnp.dot(ones.astype(BF16), before, preferred_element_type=F32)
        wanted = iota((8, length), 0).astype(F32)
        chooser = jnp.where(rank == wanted, ones, 0.0)
        return jnp.dot(chooser, records, precision=HIGHEST, preferred_element_type=F32)[:share]

    all_walls = walls[...]
    owner_all = jnp.sum(all_walls[:, size_y : size_y + 1, :], axis=0)[:, : 8 * slabs]
    cap_share = (owned_out.shape[0] - size_y) // 2
    owned_out[pl.ds(0, size_y), :] = choose(
        owner_all == (gz + 1).astype(F32), size_y, all_walls.reshape(8 * slabs, LANES)
    )
    for at in range(2):
        owned_out[pl.ds(size_y + at * cap_share, cap_share), :] = choose(
            cap_owner[pl.ds(at, 1), :] == gz, cap_share, caps[at]
        )

    def await_slope(k):
        sender = (me + peers - k) % peers

        @pl.when(sender % ratio == 0)
        def _():
            slope_copy(1, sender // ratio).wait_recv()

    each_peer(await_slope)

    def adjoint_of(j, total):
        slope = slopes[j]
        by_theta = jnp.where(sub < 4, slope[0:1], slope[4:5])
        by_phi = jnp.where(sub < 4, slope[1:2], slope[5:6])
        tiles = []
        for face in range(2):
            vector = weights[j, 2 * face] * by_theta + weights[j, 2 * face + 1] * by_phi
            turned = -sign * pltpu.roll(vector, 4, 0)
            for y in range(size_y):
                g = face * size_y + y
                tile = vector * phases[j, 0, pl.ds(g, 1), :] + turned * phases[j, 1, pl.ds(g, 1), :]
                tiles.append(jnp.concatenate([tile, -sign * pltpu.roll(tile, 4, 0)], axis=1))
        rows = jnp.concatenate(tiles, axis=0)
        high, low = split(rows)
        both = jnp.concatenate([high, low], axis=0)
        across = (((1,), (1,)), ((), ()))
        by_high = lax.dot_general(both, table_hi[j], across, preferred_element_type=F32)
        by_low = lax.dot_general(high, table_lo[j], across, preferred_element_type=F32)
        return total + by_high[:all_rows] + by_high[all_rows:] + by_low

    gradient = lax.fori_loop(0, chunks, adjoint_of, jnp.zeros((all_rows, size_x + 8 * size_z), F32))
    for y in range(size_y):
        wall = gradient[half_rows + 8 * y : half_rows + 8 * y + 8, size_x:]
        adjoint_out[pl.ds(y, 1), :] = jnp.sum(jnp.where(own_block, wall, 0.0), axis=0, keepdims=True) * norm
        cap = block_transpose(gradient[8 * y : 8 * y + 8, :size_x] * (norm * end_weight))
        adjoint_out[pl.ds(size_y + 8 * y, 8), :] = cap

    for window in range(windows):
        for copy, sends, receives in halo_copies(window):
            @pl.when(sends)
            def _():
                copy.wait_send()
    each_peer(lambda k: part_copy(k).wait_send())

    @pl.when(leads)
    def _():
        each_peer(lambda k: slope_copy(k, chunk).wait_send())

    for k in range(1, slabs):
        wall_copy(k).wait_send()
    for at, holder in enumerate((0, slabs - 1)):
        @pl.when(gz == holder)
        def _():
            for k in range(1, slabs):
                cap_copy(k, at).wait_send()


def local(fields, spectra, permittivity, phase_start, wall_owner, cap_owner, dir_index, target, aim_mask):
    slabs, devs, xys = (lax.axis_size(a) for a in ("gz", "dev", "xy"))
    peers = slabs * devs * xys
    size_y, size_z, size_x = permittivity.shape
    assert size_z == PATCH and size_x == LANES and size_y == 4
    directions = dir_index.shape[0]
    chunks = directions // LANES
    ratio = peers // chunks
    share = directions // peers
    cap_count = size_y * size_x // PATCH
    owned = size_y + 2 * (cap_count // slabs)
    rows = 16 * size_y
    depth = size_x + 8 * size_z
    windows = 2 * STEPS
    vmem, smem = (pl.BlockSpec(memory_space=s) for s in (pltpu.VMEM, pltpu.SMEM))
    dma = pltpu.SemaphoreType.DMA
    outs = pl.pallas_call(
        functools.partial(kernel, (slabs, devs, xys)),
        out_shape=(
            jax.ShapeDtypeStruct(fields.shape, F32),
            jax.ShapeDtypeStruct(spectra.shape, F32),
            jax.ShapeDtypeStruct((owned, LANES), F32),
            jax.ShapeDtypeStruct((1, LANES), F32),
            jax.ShapeDtypeStruct((size_y + cap_count, LANES), F32),
        ),
        in_specs=[vmem, vmem, vmem, smem, smem, vmem, vmem, vmem, vmem],
        out_specs=(vmem,) * 5,
        scratch_shapes=[
            pltpu.VMEM((windows, 2, size_z, LANES), F32),
            pltpu.VMEM((windows, 2, size_y, 1, LANES), F32),
            pltpu.VMEM((windows, size_z, LANES), F32),
            pltpu.VMEM((windows, 2, size_z, LANES), F32),
            pltpu.VMEM((windows, 2, size_y, 1, LANES), F32),
            pltpu.VMEM((windows, size_z, LANES), F32),
            pltpu.VMEM((8, chunks, LANES), F32),
            pltpu.VMEM((chunks, 4, 8, LANES), F32),
            pltpu.VMEM((chunks, 2, 2 * size_y, LANES), F32),
            pltpu.VMEM((chunks, depth, 2 * LANES), BF16),
            pltpu.VMEM((chunks, depth, 2 * LANES), BF16),
            pltpu.VMEM((8 * size_y, LANES), F32),
            pltpu.VMEM((2 * rows, depth), BF16),
            pltpu.VMEM((chunks, 8, LANES), F32),
            pltpu.VMEM((peers, 8, LANES), F32),
            pltpu.VMEM((chunks, 8, LANES), F32),
            pltpu.VMEM((slabs, 8, LANES), F32),
            pltpu.VMEM((2, cap_count, LANES), F32),
            dma((windows, 3)), dma((windows, 3)),
            dma((peers,)), dma((peers,)),
            dma((peers,)), dma((chunks,)),
            dma((slabs,)), dma((slabs,)),
            dma((slabs,)), dma((2,)),
        ],
        compiler_params=pltpu.CompilerParams(collective_id=0, has_side_effects=True),
    )(
        fields, spectra, permittivity, phase_start, wall_owner, cap_owner,
        dir_index.reshape(chunks, LANES), target.reshape(chunks, LANES), aim_mask.reshape(chunks, LANES),
    )
    fields_new, spectra_new, owned_rows, intensity, adjoint = outs
    intensity = intensity.reshape(LANES)
    if ratio > 1:
        me = (lax.axis_index("gz") * devs + lax.axis_index("dev")) * xys + lax.axis_index("xy")
        intensity = lax.dynamic_slice_in_dim(intensity, (me % ratio) * share, share, 0)
    return (fields_new, spectra_new, owned_rows[None, None, None], intensity, adjoint[None, None, None])


def solution(mesh):
    placed = (
        P("groups", "dev", "gz", "xy"),
        P("groups", "dev", "gz", "xy"),
        P(("groups", "dev"), "gz", "xy"),
        P("groups"),
        P("gz", None),
        P(),
        P(),
        P("groups"),
        P("groups"),
    )
    return jax.shard_map(
        local,
        mesh=mesh,
        in_specs=placed,
        out_specs=(
            P("groups", "dev", "gz", "xy"),
            P("groups", "dev", "gz", "xy"),
            P(("groups", "gz"), "dev", "xy", None, None),
            P(("groups", "gz", "dev", "xy")),
            P(("groups", "gz"), "dev", "xy", None, None),
        ),
        check_vma=False,
    )
```

```python
import functools
import math

import jax
import jax.numpy as jnp
from jax import lax
from jax.experimental import pallas as pl
from jax.experimental.pallas import tpu as pltpu
from jax.sharding import PartitionSpec as P

PATCH = 16
XB = 8
ZB = 4
STEPS = 3
THETAS = 64
COURANT = 0.5
ANGULAR_STEP = 0.3
WAVE_NUMBER = 0.6
LANES = 128
HIGHEST = lax.Precision.HIGHEST
CURRENT_SIGNS = (-1.0, 1.0, 1.0, -1.0)
X_PICKS = (5, 4, 2, 1)
Z_PICKS = (4, 3, 1, 0)
MESH = pl.DeviceIdType.MESH
AXES = ("dev", "gz", "xy")
F32 = jnp.float32
BF16 = jnp.bfloat16


def iota(shape, dim):
    return lax.broadcasted_iota(jnp.int32, shape, dim)


def sincos(turns):
    half = (turns - jnp.floor(turns + 0.5)) * math.pi
    sq = half * half
    sin_h = half * (1.0 + sq * (-1.0 / 6 + sq * (1.0 / 120 + sq * (-1.0 / 5040 + sq * (1.0 / 362880 - sq * (1.0 / 39916800))))))
    cos_h = 1.0 + sq * (-0.5 + sq * (1.0 / 24 + sq * (-1.0 / 720 + sq * (1.0 / 40320 + sq * (-1.0 / 3628800 + sq * (1.0 / 479001600))))))
    return 2.0 * sin_h * cos_h, 1.0 - 2.0 * sin_h * sin_h


def split(values):
    high = values.astype(BF16)
    return high, (values - high.astype(F32)).astype(BF16)


def block_transpose(tile):
    on_diagonal = (iota(tile.shape, 1) // PATCH) == iota(tile.shape, 0)
    total = jnp.where(on_diagonal, tile, 0.0)
    for k in range(1, 8):
        turned = pltpu.roll(tile, PATCH * k, 1)
        total = total + pltpu.roll(jnp.where(on_diagonal, turned, 0.0), 8 - k, 0)
    return total


def kernel(
    sizes,
    fields_in, spectra_in, permit_in, phase, wall_owner, cap_owner, dirs, target, aim,
    fields_out, spectra_out, owned_out, intensity_out, adjoint_out,
    send_y, send_z, send_x, got_y, got_z, got_x,
    fields, spectra, permit, geo, weights, phases, table_hi, table_lo, cap_plane, lhs,
    parts_out, parts_in, slopes, walls, caps,
    halo_send, halo_got, part_send, part_got, slope_send, slope_got, wall_send, wall_got, cap_send, cap_got, loads,
):
    slabs, devs, xys = sizes
    peers = slabs * devs * xys
    size_y, size_z, size_x = permit.shape
    chunks = dirs.shape[0]
    ratio = peers // chunks
    groups = 2 * size_y
    half_rows = 8 * size_y
    all_rows = 2 * half_rows
    gz, dev, xy = lax.axis_index("gz"), lax.axis_index("dev"), lax.axis_index("xy")
    me = (gz * devs + dev) * xys + xy
    place = {"dev": dev, "gz": gz, "xy": xy}
    count = {"dev": devs, "gz": slabs, "xy": xys}

    loading = [
        pltpu.make_async_copy(source, held, loads.at[number])
        for number, (source, held) in enumerate(((fields_in, fields), (permit_in, permit), (spectra_in, spectra)))
    ]
    for copy in loading:
        copy.start()

    def ident(flat):
        return {"gz": flat // (devs * xys), "dev": (flat // xys) % devs, "xy": flat % xys}

    barrier = pltpu.get_barrier_semaphore()

    def greet(k, carry):
        pl.semaphore_signal(barrier, inc=1, device_id=ident((me + k) % peers), device_id_type=MESH)
        return carry

    lax.fori_loop(1, peers, greet, 0)

    index = dirs[...]
    sin_t, cos_t = sincos(((index // THETAS).astype(F32) + 0.5) * (0.5 / THETAS))
    sin_f, cos_f = sincos((index % THETAS).astype(F32) * (1.0 / THETAS))
    wave = WAVE_NUMBER / (2.0 * math.pi)
    for slot, values in enumerate((
        wave * sin_t * cos_f, wave * sin_t * sin_f, wave * cos_t,
        cos_t * cos_f, cos_t * sin_f, -sin_t, -sin_f, cos_f,
    )):
        geo[slot] = values

    grid_x, grid_y, grid_z = size_x * xys, size_y * devs, size_z * slabs
    x_first = (xy * size_x).astype(F32) - (grid_x - 1) / 2.0
    y_first = (dev * size_y).astype(F32) - (grid_y - 1) / 2.0
    z_first = (gz * size_z).astype(F32) - (grid_z - 1) / 2.0
    x_wall = jnp.where(xy == 0, XB, size_x - 1 - XB)
    z_cap = jnp.where(gz == 0, ZB, size_z - 1 - ZB)
    x_face = x_first + x_wall.astype(F32)
    z_face = z_first + z_cap.astype(F32)
    facing_x = jnp.where(xy == 0, -1.0, 1.0)
    facing_z = jnp.where(gz == 0, -1.0, 1.0)
    is_end = jnp.logical_or(gz == 0, gz == slabs - 1)
    end_weight = jnp.where(is_end, 1.0, 0.0)
    norm = 1.0 / math.sqrt(2.0 * (2 * grid_y * grid_z + 2 * grid_y * grid_x))

    def make_tables(j, carry):
        def row(slot):
            return geo[slot, pl.ds(j, 1), :]

        ux, uy, uz = row(0), row(1), row(2)
        blocks = size_x // 8
        far_s, far_c = sincos((iota((blocks, LANES), 0).astype(F32) * 8.0 + x_first) * ux)
        near_s, near_c = sincos(iota((8, LANES), 0).astype(F32) * ux)
        far_s, far_c = far_s[:, None, :], far_c[:, None, :]
        near_s, near_c = near_s[None], near_c[None]
        cos_x = (far_c * near_c - far_s * near_s).reshape(size_x, LANES)
        sin_x = (far_s * near_c + far_c * near_s).reshape(size_x, LANES)
        sin_z, cos_z = sincos((iota((size_z, LANES), 0).astype(F32) + z_first) * uz)
        for at, (x_part, z_part) in enumerate(((cos_x, cos_z), (sin_x, sin_z))):
            lanes = pl.ds(at * LANES, LANES)
            x_high, x_low = split(x_part)
            z_high, z_low = split(z_part)
            table_hi[j, pl.ds(0, size_x), lanes] = x_high
            table_lo[j, pl.ds(0, size_x), lanes] = x_low
            table_hi[j, pl.ds(size_x, 8 * size_z), lanes] = jnp.concatenate([z_high] * 8, axis=0)
            table_lo[j, pl.ds(size_x, 8 * size_z), lanes] = jnp.concatenate([z_low] * 8, axis=0)
        which = iota((groups, LANES), 0)
        cell_y = (which % size_y).astype(F32) + y_first
        sin_g, cos_g = sincos(cell_y * uy + jnp.where(which < size_y, z_face * uz, x_face * ux))
        phases[j, 0] = cos_g
        phases[j, 1] = sin_g
        kind = iota((8, LANES), 0) % 4

        def pattern(a, b, c, d):
            return jnp.where(kind == 0, a, jnp.where(kind == 1, b, jnp.where(kind == 2, c, d)))

        tx, ty, tz, fx, fy = row(3), row(4), row(5), row(6), row(7)
        weights[j, 0] = pattern(-tx, -ty, -fx, -fy)
        weights[j, 1] = pattern(-fx, -fy, tx, ty)
        weights[j, 2] = pattern(-ty, -tz, -fy, jnp.zeros_like(fy))
        weights[j, 3] = pattern(-fy, jnp.zeros_like(fy), ty, tz)
        return carry

    windows = 2 * STEPS

    def tables_of(window):
        lax.fori_loop(window * chunks // windows, (window + 1) * chunks // windows, make_tables, 0)

    order = iota((8, LANES), 0).astype(F32)
    run_s, run_c = sincos((phase[0] + 0.5 * ANGULAR_STEP * (order + 1.0)) * (0.5 / math.pi))

    for number, (axis, got) in enumerate(zip(AXES, (got_y, got_z, got_x))):
        @pl.when(place[axis] == count[axis] - 1)
        def _():
            for window in range(0, windows, 2):
                got[window] = jnp.zeros(got.shape[1:], F32)

        @pl.when(place[axis] == 0)
        def _():
            for window in range(1, windows, 2):
                got[window] = jnp.zeros(got.shape[1:], F32)

    loading[0].wait()
    pl.semaphore_wait(barrier, peers - 1)

    lane = iota((size_z, LANES), 1)
    lane3 = iota((size_y, size_z, LANES), 2)
    row3 = iota((size_y, size_z, LANES), 1)

    def halo_copies(window):
        step = -1 if window % 2 == 0 else 1
        copies = []
        for number, (axis, source, landing) in enumerate(
            zip(AXES, (send_y, send_z, send_x), (got_y, got_z, got_x))
        ):
            mine, total = place[axis], count[axis]
            copy = pltpu.make_async_remote_copy(
                src_ref=source.at[window],
                dst_ref=landing.at[window],
                send_sem=halo_send.at[window, number],
                recv_sem=halo_got.at[window, number],
                device_id={axis: (mine + step + total) % total},
                device_id_type=MESH,
            )
            if step < 0:
                copies.append((copy, mine > 0, mine < total - 1))
            else:
                copies.append((copy, mine < total - 1, mine > 0))
        return copies

    def start_halo(window, for_y, for_z, for_x):
        ahead = window % 2 == 0
        at_y, at_z = (0, 0) if ahead else (size_y - 1, size_z - 1)
        for k in range(2):
            send_y[window, k] = for_y[k][at_y]
            send_z[window, k] = for_z[k][:, at_z : at_z + 1, :]
        packed = jnp.zeros((size_z, LANES), F32)
        for k in range(2):
            for y in range(size_y):
                spot = k * size_y + y
                amount = spot if ahead else (spot + 1) % LANES
                value = for_x[k][y]
                turned = pltpu.roll(value, amount, 1) if amount else value
                packed = jnp.where(lane == spot, turned, packed)
        send_x[window] = packed
        for copy, sends, receives in halo_copies(window):
            @pl.when(sends)
            def _():
                copy.start()

    def wait_halo(window):
        for copy, sends, receives in halo_copies(window):
            @pl.when(receives)
            def _():
                copy.wait_recv()

    def shift_y(window, k, value):
        other = got_y[window, k][None]
        if window % 2 == 0:
            return jnp.concatenate([value[1:], other], axis=0) - value
        return value - jnp.concatenate([other, value[:-1]], axis=0)

    def shift_z(window, k, value):
        other = got_z[window, k]
        if window % 2 == 0:
            return jnp.where(row3 == size_z - 1, other, pltpu.roll(value, size_z - 1, 1)) - value
        return value - jnp.where(row3 == 0, other, pltpu.roll(value, 1, 1))

    def shift_x(window, k, value):
        landed = got_x[window]
        edges = []
        for y in range(size_y):
            spot = k * size_y + y
            if window % 2 == 0:
                edges.append(pltpu.roll(landed, LANES - 1 - spot, 1))
            else:
                amount = (LANES - spot) % LANES
                edges.append(pltpu.roll(landed, amount, 1) if amount else landed)
        other = jnp.stack(edges, axis=0)
        if window % 2 == 0:
            return jnp.where(lane3 == size_x - 1, other, pltpu.roll(value, size_x - 1, 2)) - value
        return value - jnp.where(lane3 == 0, other, pltpu.roll(value, 1, 2))

    ex, ey, ez = fields[0], fields[1], fields[2]
    start_halo(0, (ez, ex), (ey, ex), (ez, ey))
    loading[1].wait()
    rate = COURANT / permit[...]
    loading[2].wait()
    hx, hy, hz = fields[3], fields[4], fields[5]
    spec_from = spectra
    for n in range(STEPS):
        window = 2 * n
        tables_of(window)
        wait_halo(window)
        hx = hx - COURANT * (shift_y(window, 0, ez) - shift_z(window, 0, ey))
        hy = hy - COURANT * (shift_z(window, 1, ex) - shift_x(window, 0, ez))
        hz = hz - COURANT * (shift_x(window, 1, ey) - shift_y(window, 1, ex))
        window = 2 * n + 1
        start_halo(window, (hz, hx), (hy, hx), (hz, hy))
        half_c, half_s = run_c[2 * n : 2 * n + 1, :], run_s[2 * n : 2 * n + 1, :]
        for c, value in enumerate((hx, hy, hz)):
            spectra_out[3 + c] = spec_from[3 + c] + value * half_c
            spectra_out[9 + c] = spec_from[9 + c] - value * half_s
        tables_of(window)
        wait_halo(window)
        ex = ex + rate * (shift_y(window, 0, hz) - shift_z(window, 0, hy))
        ey = ey + rate * (shift_z(window, 1, hx) - shift_x(window, 0, hz))
        ez = ez + rate * (shift_x(window, 1, hy) - shift_y(window, 1, hx))
        if n < STEPS - 1:
            start_halo(window + 1, (ez, ex), (ey, ex), (ez, ey))
        full_c, full_s = run_c[2 * n + 1 : 2 * n + 2, :], run_s[2 * n + 1 : 2 * n + 2, :]
        for c, value in enumerate((ex, ey, ez)):
            spectra_out[c] = spec_from[c] + value * full_c
            spectra_out[6 + c] = spec_from[6 + c] - value * full_s
        spec_from = spectra_out
    for c, value in enumerate((ex, ey, ez, hx, hy, hz)):
        fields_out[c] = value

    own_walls = walls.at[gz]
    lane_block = iota((8, LANES), 1) // PATCH
    sub = iota((8, LANES), 0)
    own_block = lane_block == sub
    z_row = iota((size_z, LANES), 0)
    own_walls[...] = jnp.zeros((8, LANES), F32)
    for y in range(size_y):
        spread = jnp.zeros((size_z, LANES), F32)
        for c in range(8):
            k = c % 4
            from_c = X_PICKS[k] + (6 if c >= 4 else 0)
            column = jnp.sum(jnp.where(lane == x_wall, spectra_out[from_c, y], 0.0), axis=1, keepdims=True)
            spread = jnp.where(lane == c * PATCH + z_row, column * (CURRENT_SIGNS[k] * facing_x), spread)
        record = jnp.sum(spread, axis=0, keepdims=True)
        own_walls[pl.ds(y, 1), :] = record
        for c in range(8):
            k = c % 4
            from_c = Z_PICKS[k] + (6 if c >= 4 else 0)
            low = spectra_out[from_c, y, pl.ds(ZB, 1), :]
            high = spectra_out[from_c, y, pl.ds(size_z - 1 - ZB, 1), :]
            picked = jnp.where(gz == 0, low, high) * (CURRENT_SIGNS[k] * facing_z * end_weight)
            cap_plane[pl.ds(8 * y + c, 1), :] = picked
        wall_hi, wall_lo = split(jnp.where(own_block, record, 0.0) * norm)
        cap_hi, cap_lo = split(cap_plane[pl.ds(8 * y, 8), :] * norm)
        none = jnp.zeros((8, LANES), BF16)
        for at, (cap_part, wall_part) in enumerate(((cap_hi, wall_hi), (cap_lo, wall_lo))):
            first = at * all_rows + 8 * y
            lhs[pl.ds(first, 8), :] = jnp.concatenate([cap_part, none], axis=1)
            lhs[pl.ds(first + half_rows, 8), :] = jnp.concatenate([none, wall_part], axis=1)

    lanes8 = iota((1, LANES), 1)
    owner_row = jnp.zeros((1, LANES), F32)
    for p in range(size_y):
        owner_row = jnp.where(lanes8 == 8 * gz + p, (wall_owner[0, p] + 1).astype(F32), owner_row)
    own_walls[pl.ds(size_y, 1), :] = owner_row

    def wall_copy(k):
        return pltpu.make_async_remote_copy(
            src_ref=walls.at[gz],
            dst_ref=walls.at[gz],
            send_sem=wall_send.at[k],
            recv_sem=wall_got.at[gz],
            device_id={"gz": (gz + k) % slabs},
            device_id_type=MESH,
        )

    def wall_landing(s):
        return pltpu.make_async_remote_copy(
            src_ref=walls.at[s], dst_ref=walls.at[s], send_sem=wall_send.at[0], recv_sem=wall_got.at[s],
            device_id={"gz": (gz + 1) % slabs}, device_id_type=MESH,
        )

    def cap_copy(k, at):
        return pltpu.make_async_remote_copy(
            src_ref=caps.at[at],
            dst_ref=caps.at[at],
            send_sem=cap_send.at[k],
            recv_sem=cap_got.at[at],
            device_id={"gz": (gz + k) % slabs},
            device_id_type=MESH,
        )

    for k in range(1, slabs):
        wall_copy(k).start()
    for at, holder in enumerate((0, slabs - 1)):
        @pl.when(gz == holder)
        def _():
            for y in range(size_y):
                caps[at, pl.ds(8 * y, 8), :] = block_transpose(cap_plane[pl.ds(8 * y, 8), :])
            for k in range(1, slabs):
                cap_copy(k, at).start()

    sign = jnp.where(sub < 4, -1.0, 1.0)

    def far_of(j):
        rows = lhs[...]
        by_high = jnp.dot(rows, table_hi[j], preferred_element_type=F32)
        by_low = jnp.dot(rows[:all_rows], table_lo[j], preferred_element_type=F32)
        product = by_high[:all_rows] + by_high[all_rows:] + by_low
        theta = jnp.zeros((8, LANES), F32)
        phi = jnp.zeros((8, LANES), F32)
        for face in range(2):
            sum_c = jnp.zeros((8, LANES), F32)
            sum_s = jnp.zeros((8, LANES), F32)
            for y in range(size_y):
                g = face * size_y + y
                tile = product[8 * g : 8 * g + 8]
                tile = tile[:, :LANES] + sign * pltpu.roll(tile[:, LANES:], 4, 0)
                sum_c = sum_c + tile * phases[j, 0, pl.ds(g, 1), :]
                sum_s = sum_s + tile * phases[j, 1, pl.ds(g, 1), :]
            far = sum_c + sign * pltpu.roll(sum_s, 4, 0)
            theta = theta + weights[j, 2 * face] * far
            phi = phi + weights[j, 2 * face + 1] * far

        def four(values):
            pairs = values + pltpu.roll(values, 7, 0)
            return pairs + pltpu.roll(pairs, 6, 0)

        parts_out[j] = jnp.where(sub % 4 == 1, pltpu.roll(four(phi), 1, 0), four(theta))

    chunk = me // ratio

    def partner(number):
        other, bit = 0, 1
        while bit < chunks:
            other = other + bit * ((chunk // bit + number // bit) % 2)
            bit *= 2
        return other

    def part_copy(k):
        peer = (me + k) % peers
        return pltpu.make_async_remote_copy(
            src_ref=parts_out.at[peer // ratio],
            dst_ref=parts_in.at[k],
            send_sem=part_send.at[k],
            recv_sem=part_got.at[k],
            device_id=ident(peer),
            device_id_type=MESH,
        )

    def each_peer(act):
        def body(k, carry):
            act(k)
            return carry

        lax.fori_loop(1, peers, body, 0)

    def far_and_send(number, carry):
        to = partner(chunks - 1 - number)
        far_of(to)
        for r in range(ratio):
            peer = to * ratio + r

            @pl.when(peer != me)
            def _():
                part_copy((peer - me + peers) % peers).start()

        return carry

    lax.fori_loop(0, chunks, far_and_send, 0)
    parts_in[0] = parts_out[chunk]

    for s in range(slabs):
        @pl.when(s != gz)
        def _():
            wall_landing(s).wait_recv()
    for at, holder in enumerate((0, slabs - 1)):
        @pl.when(gz != holder)
        def _():
            cap_copy(1, at).wait_recv()

    def choose(mine, share, records):
        length = mine.shape[1]
        before = jnp.where(iota((length, length), 0) < iota((length, length), 1), 1.0, 0.0).astype(BF16)
        ones = jnp.broadcast_to(jnp.where(mine, 1.0, 0.0), (8, length))
        rank = jnp.dot(ones.astype(BF16), before, preferred_element_type=F32)
        wanted = iota((8, length), 0).astype(F32)
        chooser = jnp.where(rank == wanted, ones, 0.0)
        return jnp.dot(chooser, records, precision=HIGHEST, preferred_element_type=F32)[:share]

    all_walls = walls[...]
    owner_all = jnp.sum(all_walls[:, size_y : size_y + 1, :], axis=0)[:, : 8 * slabs]
    cap_share = (owned_out.shape[0] - size_y) // 2
    owned_out[pl.ds(0, size_y), 0, :] = choose(
        owner_all == (gz + 1).astype(F32), size_y, all_walls.reshape(8 * slabs, LANES)
    )
    for at in range(2):
        owned_out[pl.ds(size_y + at * cap_share, cap_share), 0, :] = choose(
            cap_owner[pl.ds(at, 1), :] == gz, cap_share, caps[at]
        )

    each_peer(lambda k: part_copy(k).wait_recv())
    field = jnp.sum(parts_in[...], axis=0)
    power = jnp.where(sub % 4 < 2, field * field, 0.0)
    intensity = jnp.sum(power, axis=0, keepdims=True)
    intensity_out[...] = intensity
    residual = aim[pl.ds(chunk, 1), :].astype(F32) * (intensity - target[pl.ds(chunk, 1), :])
    leads = me % ratio == 0

    def slope_copy(k, of):
        return pltpu.make_async_remote_copy(
            src_ref=slopes.at[of],
            dst_ref=slopes.at[of],
            send_sem=slope_send.at[k],
            recv_sem=slope_got.at[of],
            device_id=ident((me + k) % peers),
            device_id_type=MESH,
        )

    @pl.when(leads)
    def _():
        slopes[chunk] = 2.0 * residual * field
        each_peer(lambda k: slope_copy(k, chunk).start())

    def adjoint_of(number, total):
        j = partner(number)

        @pl.when(j * ratio != me)
        def _():
            slope_copy(1, j).wait_recv()

        slope = slopes[j]
        by_theta = jnp.where(sub < 4, slope[0:1], slope[4:5])
        by_phi = jnp.where(sub < 4, slope[1:2], slope[5:6])
        tiles = []
        for face in range(2):
            vector = weights[j, 2 * face] * by_theta + weights[j, 2 * face + 1] * by_phi
            turned = -sign * pltpu.roll(vector, 4, 0)
            for y in range(size_y):
                g = face * size_y + y
                tile = vector * phases[j, 0, pl.ds(g, 1), :] + turned * phases[j, 1, pl.ds(g, 1), :]
                tiles.append(jnp.concatenate([tile, -sign * pltpu.roll(tile, 4, 0)], axis=1))
        rows = jnp.concatenate(tiles, axis=0)
        high, low = split(rows)
        both = jnp.concatenate([high, low], axis=0)
        across = (((1,), (1,)), ((), ()))
        by_high = lax.dot_general(both, table_hi[j], across, preferred_element_type=F32)
        by_low = lax.dot_general(high, table_lo[j], across, preferred_element_type=F32)
        return total + by_high[:all_rows] + by_high[all_rows:] + by_low

    gradient = lax.fori_loop(0, chunks, adjoint_of, jnp.zeros((all_rows, size_x + 8 * size_z), F32))
    for y in range(size_y):
        wall = gradient[half_rows + 8 * y : half_rows + 8 * y + 8, size_x:]
        adjoint_out[pl.ds(y, 1), 0, :] = jnp.sum(jnp.where(own_block, wall, 0.0), axis=0, keepdims=True) * norm
        cap = block_transpose(gradient[8 * y : 8 * y + 8, :size_x] * (norm * end_weight))
        adjoint_out[pl.ds(size_y + 8 * y, 8), 0, :] = cap

    for window in range(windows):
        for copy, sends, receives in halo_copies(window):
            @pl.when(sends)
            def _():
                copy.wait_send()
    each_peer(lambda k: part_copy(k).wait_send())

    @pl.when(leads)
    def _():
        each_peer(lambda k: slope_copy(k, chunk).wait_send())

    for k in range(1, slabs):
        wall_copy(k).wait_send()
    for at, holder in enumerate((0, slabs - 1)):
        @pl.when(gz == holder)
        def _():
            for k in range(1, slabs):
                cap_copy(k, at).wait_send()


def write_out(*refs):
    copies = [pltpu.make_async_copy(refs[i], refs[5 + i], refs[10].at[i]) for i in range(5)]
    for copy in copies:
        copy.start()
    for copy in copies:
        copy.wait()


def local(fields, spectra, permittivity, phase_start, wall_owner, cap_owner, dir_index, target, aim_mask):
    slabs, devs, xys = (lax.axis_size(a) for a in ("gz", "dev", "xy"))
    peers = slabs * devs * xys
    size_y, size_z, size_x = permittivity.shape
    assert size_z == PATCH and size_x == LANES and size_y == 4
    directions = dir_index.shape[0]
    chunks = directions // LANES
    ratio = peers // chunks
    share = directions // peers
    cap_count = size_y * size_x // PATCH
    owned = size_y + 2 * (cap_count // slabs)
    rows = 16 * size_y
    depth = size_x + 8 * size_z
    windows = 2 * STEPS
    vmem, smem = (pl.BlockSpec(memory_space=s) for s in (pltpu.VMEM, pltpu.SMEM))
    anywhere = pl.BlockSpec(memory_space=pl.ANY)
    dma = pltpu.SemaphoreType.DMA
    outs = pl.pallas_call(
        functools.partial(kernel, (slabs, devs, xys)),
        out_shape=(
            pltpu.VMEM(fields.shape, F32),
            pltpu.VMEM(spectra.shape, F32),
            pltpu.VMEM((owned, 1, LANES), F32),
            pltpu.VMEM((1, LANES), F32),
            pltpu.VMEM((size_y + cap_count, 1, LANES), F32),
        ),
        in_specs=[anywhere, anywhere, anywhere, smem, smem, vmem, vmem, vmem, vmem],
        out_specs=(vmem,) * 5,
        scratch_shapes=[
            pltpu.VMEM((windows, 2, size_z, LANES), F32),
            pltpu.VMEM((windows, 2, size_y, 1, LANES), F32),
            pltpu.VMEM((windows, size_z, LANES), F32),
            pltpu.VMEM((windows, 2, size_z, LANES), F32),
            pltpu.VMEM((windows, 2, size_y, 1, LANES), F32),
            pltpu.VMEM((windows, size_z, LANES), F32),
            pltpu.VMEM(fields.shape, F32),
            pltpu.VMEM(spectra.shape, F32),
            pltpu.VMEM(permittivity.shape, F32),
            pltpu.VMEM((8, chunks, LANES), F32),
            pltpu.VMEM((chunks, 4, 8, LANES), F32),
            pltpu.VMEM((chunks, 2, 2 * size_y, LANES), F32),
            pltpu.VMEM((chunks, depth, 2 * LANES), BF16),
            pltpu.VMEM((chunks, depth, 2 * LANES), BF16),
            pltpu.VMEM((8 * size_y, LANES), F32),
            pltpu.VMEM((2 * rows, depth), BF16),
            pltpu.VMEM((chunks, 8, LANES), F32),
            pltpu.VMEM((peers, 8, LANES), F32),
            pltpu.VMEM((chunks, 8, LANES), F32),
            pltpu.VMEM((slabs, 8, LANES), F32),
            pltpu.VMEM((2, cap_count, LANES), F32),
            dma((windows, 3)), dma((windows, 3)),
            dma((peers,)), dma((peers,)),
            dma((peers,)), dma((chunks,)),
            dma((slabs,)), dma((slabs,)),
            dma((slabs,)), dma((2,)),
            dma((3,)),
        ],
        compiler_params=pltpu.CompilerParams(collective_id=0, has_side_effects=True),
    )(
        fields, spectra, permittivity, phase_start, wall_owner, cap_owner,
        dir_index.reshape(chunks, LANES), target.reshape(chunks, LANES), aim_mask.reshape(chunks, LANES),
    )
    held = (fields.shape, spectra.shape, (owned, 1, LANES), (1, LANES), (size_y + cap_count, 1, LANES))
    fields_new, spectra_new, owned_rows, intensity, adjoint = pl.pallas_call(
        write_out,
        out_shape=tuple(jax.ShapeDtypeStruct(shape, F32) for shape in held),
        in_specs=[pl.BlockSpec(memory_space=pltpu.VMEM)] * 5,
        out_specs=(pl.BlockSpec(memory_space=pl.ANY),) * 5,
        scratch_shapes=[dma((5,))],
    )(*(pltpu.with_memory_space_constraint(out, pltpu.VMEM) for out in outs))
    owned_rows = owned_rows.reshape(1, 1, owned, 1, LANES).transpose(0, 1, 3, 2, 4)
    adjoint = adjoint.reshape(1, 1, size_y + cap_count, 1, LANES).transpose(0, 1, 3, 2, 4)
    intensity = intensity.reshape(LANES)
    if ratio > 1:
        me = (lax.axis_index("gz") * devs + lax.axis_index("dev")) * xys + lax.axis_index("xy")
        intensity = lax.dynamic_slice_in_dim(intensity, (me % ratio) * share, share, 0)
    return (fields_new, spectra_new, owned_rows, intensity, adjoint)


def solution(mesh):
    placed = (
        P("groups", "dev", "gz", "xy"),
        P("groups", "dev", "gz", "xy"),
        P(("groups", "dev"), "gz", "xy"),
        P("groups"),
        P("gz", None),
        P(),
        P(),
        P("groups"),
        P("groups"),
    )
    return jax.shard_map(
        local,
        mesh=mesh,
        in_specs=placed,
        out_specs=(
            P("groups", "dev", "gz", "xy"),
            P("groups", "dev", "gz", "xy"),
            P(("groups", "gz"), "dev", "xy", None, None),
            P(("groups", "gz", "dev", "xy")),
            P(("groups", "gz"), "dev", "xy", None, None),
        ),
        check_vma=False,
    )
```

```python
import functools
import math

import jax
import jax.numpy as jnp
from jax import lax
from jax.experimental import pallas as pl
from jax.experimental.pallas import tpu as pltpu
from jax.sharding import PartitionSpec as P

PATCH = 16
XB = 8
ZB = 4
STEPS = 3
THETAS = 64
COURANT = 0.5
ANGULAR_STEP = 0.3
WAVE_NUMBER = 0.6
LANES = 128
HIGHEST = lax.Precision.HIGHEST
CURRENT_SIGNS = (-1.0, 1.0, 1.0, -1.0)
X_PICKS = (5, 4, 2, 1)
Z_PICKS = (4, 3, 1, 0)
MESH = pl.DeviceIdType.MESH
AXES = ("dev", "gz", "xy")
F32 = jnp.float32
BF16 = jnp.bfloat16


def iota(shape, dim):
    return lax.broadcasted_iota(jnp.int32, shape, dim)


def sincos(turns):
    half = (turns - jnp.floor(turns + 0.5)) * math.pi
    sq = half * half
    sin_h = half * (1.0 + sq * (-1.0 / 6 + sq * (1.0 / 120 + sq * (-1.0 / 5040 + sq * (1.0 / 362880 - sq * (1.0 / 39916800))))))
    cos_h = 1.0 + sq * (-0.5 + sq * (1.0 / 24 + sq * (-1.0 / 720 + sq * (1.0 / 40320 + sq * (-1.0 / 3628800 + sq * (1.0 / 479001600))))))
    return 2.0 * sin_h * cos_h, 1.0 - 2.0 * sin_h * sin_h


def split(values):
    high = values.astype(BF16)
    return high, (values - high.astype(F32)).astype(BF16)


def block_transpose(tile):
    on_diagonal = (iota(tile.shape, 1) // PATCH) == iota(tile.shape, 0)
    total = jnp.where(on_diagonal, tile, 0.0)
    for k in range(1, 8):
        turned = pltpu.roll(tile, PATCH * k, 1)
        total = total + pltpu.roll(jnp.where(on_diagonal, turned, 0.0), 8 - k, 0)
    return total


def kernel(
    sizes,
    fields_in, spectra_in, permit_in, phase, wall_owner, cap_owner, dirs, target, aim,
    fields_out, spectra_out, owned_out, intensity_out, adjoint_out,
    send_y, send_z, send_x, got_y, got_z, got_x,
    fields, spectra, permit, geo, weights, phases, table_hi, table_lo, cap_plane, lhs,
    parts_out, parts_in, slopes, walls, caps,
    halo_send, halo_got, part_send, part_got, slope_send, slope_got, wall_send, wall_got, cap_send, cap_got, loads,
):
    slabs, devs, xys = sizes
    peers = slabs * devs * xys
    size_y, size_z, size_x = permit.shape
    chunks = dirs.shape[0]
    ratio = peers // chunks
    groups = 2 * size_y
    half_rows = 8 * size_y
    all_rows = 2 * half_rows
    gz, dev, xy = lax.axis_index("gz"), lax.axis_index("dev"), lax.axis_index("xy")
    me = (gz * devs + dev) * xys + xy
    place = {"dev": dev, "gz": gz, "xy": xy}
    count = {"dev": devs, "gz": slabs, "xy": xys}

    loading = [
        pltpu.make_async_copy(source, held, loads.at[number])
        for number, (source, held) in enumerate(((fields_in, fields), (permit_in, permit), (spectra_in, spectra)))
    ]
    for copy in loading:
        copy.start()

    def ident(flat):
        return {"gz": flat // (devs * xys), "dev": (flat // xys) % devs, "xy": flat % xys}

    barrier = pltpu.get_barrier_semaphore()

    def greet(k, carry):
        pl.semaphore_signal(barrier, inc=1, device_id=ident((me + k) % peers), device_id_type=MESH)
        return carry

    lax.fori_loop(1, peers, greet, 0)

    index = dirs[...]
    sin_t, cos_t = sincos(((index // THETAS).astype(F32) + 0.5) * (0.5 / THETAS))
    sin_f, cos_f = sincos((index % THETAS).astype(F32) * (1.0 / THETAS))
    wave = WAVE_NUMBER / (2.0 * math.pi)
    for slot, values in enumerate((
        wave * sin_t * cos_f, wave * sin_t * sin_f, wave * cos_t,
        cos_t * cos_f, cos_t * sin_f, -sin_t, -sin_f, cos_f,
    )):
        geo[slot] = values

    grid_x, grid_y, grid_z = size_x * xys, size_y * devs, size_z * slabs
    x_first = (xy * size_x).astype(F32) - (grid_x - 1) / 2.0
    y_first = (dev * size_y).astype(F32) - (grid_y - 1) / 2.0
    z_first = (gz * size_z).astype(F32) - (grid_z - 1) / 2.0
    x_wall = jnp.where(xy == 0, XB, size_x - 1 - XB)
    z_cap = jnp.where(gz == 0, ZB, size_z - 1 - ZB)
    x_face = x_first + x_wall.astype(F32)
    z_face = z_first + z_cap.astype(F32)
    facing_x = jnp.where(xy == 0, -1.0, 1.0)
    facing_z = jnp.where(gz == 0, -1.0, 1.0)
    is_end = jnp.logical_or(gz == 0, gz == slabs - 1)
    end_weight = jnp.where(is_end, 1.0, 0.0)
    norm = 1.0 / math.sqrt(2.0 * (2 * grid_y * grid_z + 2 * grid_y * grid_x))

    def make_tables(j, carry):
        def row(slot):
            return geo[slot, pl.ds(j, 1), :]

        ux, uy, uz = row(0), row(1), row(2)
        blocks = size_x // 8
        far_s, far_c = sincos((iota((blocks, LANES), 0).astype(F32) * 8.0 + x_first) * ux)
        near_s, near_c = sincos(iota((8, LANES), 0).astype(F32) * ux)
        far_s, far_c = far_s[:, None, :], far_c[:, None, :]
        near_s, near_c = near_s[None], near_c[None]
        cos_x = (far_c * near_c - far_s * near_s).reshape(size_x, LANES)
        sin_x = (far_s * near_c + far_c * near_s).reshape(size_x, LANES)
        sin_z, cos_z = sincos((iota((size_z, LANES), 0).astype(F32) + z_first) * uz)
        for at, (x_part, z_part) in enumerate(((cos_x, cos_z), (sin_x, sin_z))):
            lanes = pl.ds(at * LANES, LANES)
            x_high, x_low = split(x_part)
            z_high, z_low = split(z_part)
            table_hi[j, pl.ds(0, size_x), lanes] = x_high
            table_lo[j, pl.ds(0, size_x), lanes] = x_low
            table_hi[j, pl.ds(size_x, 8 * size_z), lanes] = jnp.concatenate([z_high] * 8, axis=0)
            table_lo[j, pl.ds(size_x, 8 * size_z), lanes] = jnp.concatenate([z_low] * 8, axis=0)
        which = iota((groups, LANES), 0)
        cell_y = (which % size_y).astype(F32) + y_first
        sin_g, cos_g = sincos(cell_y * uy + jnp.where(which < size_y, z_face * uz, x_face * ux))
        phases[j, 0] = cos_g
        phases[j, 1] = sin_g
        kind = iota((8, LANES), 0) % 4

        def pattern(a, b, c, d):
            return jnp.where(kind == 0, a, jnp.where(kind == 1, b, jnp.where(kind == 2, c, d)))

        tx, ty, tz, fx, fy = row(3), row(4), row(5), row(6), row(7)
        weights[j, 0] = pattern(-tx, -ty, -fx, -fy)
        weights[j, 1] = pattern(-fx, -fy, tx, ty)
        weights[j, 2] = pattern(-ty, -tz, -fy, jnp.zeros_like(fy))
        weights[j, 3] = pattern(-fy, jnp.zeros_like(fy), ty, tz)
        return carry

    windows = 2 * STEPS

    def tables_of(window):
        lax.fori_loop(window * chunks // windows, (window + 1) * chunks // windows, make_tables, 0)

    order = iota((8, LANES), 0).astype(F32)
    run_s, run_c = sincos((phase[...] + 0.5 * ANGULAR_STEP * (order + 1.0)) * (0.5 / math.pi))

    for number, (axis, got) in enumerate(zip(AXES, (got_y, got_z, got_x))):
        @pl.when(place[axis] == count[axis] - 1)
        def _():
            for window in range(0, windows, 2):
                got[window] = jnp.zeros(got.shape[1:], F32)

        @pl.when(place[axis] == 0)
        def _():
            for window in range(1, windows, 2):
                got[window] = jnp.zeros(got.shape[1:], F32)

    loading[0].wait()
    pl.semaphore_wait(barrier, peers - 1)

    lane = iota((size_z, LANES), 1)
    lane3 = iota((size_y, size_z, LANES), 2)
    row3 = iota((size_y, size_z, LANES), 1)

    def halo_copies(window):
        step = -1 if window % 2 == 0 else 1
        copies = []
        for number, (axis, source, landing) in enumerate(
            zip(AXES, (send_y, send_z, send_x), (got_y, got_z, got_x))
        ):
            mine, total = place[axis], count[axis]
            copy = pltpu.make_async_remote_copy(
                src_ref=source.at[window],
                dst_ref=landing.at[window],
                send_sem=halo_send.at[window, number],
                recv_sem=halo_got.at[window, number],
                device_id={axis: (mine + step + total) % total},
                device_id_type=MESH,
            )
            if step < 0:
                copies.append((copy, mine > 0, mine < total - 1))
            else:
                copies.append((copy, mine < total - 1, mine > 0))
        return copies

    def start_halo(window, for_y, for_z, for_x):
        ahead = window % 2 == 0
        at_y, at_z = (0, 0) if ahead else (size_y - 1, size_z - 1)
        for k in range(2):
            send_y[window, k] = for_y[k][at_y]
            send_z[window, k] = for_z[k][:, at_z : at_z + 1, :]
        copies = halo_copies(window)
        for copy, sends, receives in copies[:2]:
            @pl.when(sends)
            def _():
                copy.start()
        packed = jnp.zeros((size_z, LANES), F32)
        for k in range(2):
            for y in range(size_y):
                spot = k * size_y + y
                amount = spot if ahead else (spot + 1) % LANES
                value = for_x[k][y]
                turned = pltpu.roll(value, amount, 1) if amount else value
                packed = jnp.where(lane == spot, turned, packed)
        send_x[window] = packed
        copy, sends, receives = copies[2]

        @pl.when(sends)
        def _():
            copy.start()

    def wait_halo(window):
        for copy, sends, receives in halo_copies(window):
            @pl.when(receives)
            def _():
                copy.wait_recv()

    def inner(ahead, axis, value):
        if axis == 0:
            none = jnp.zeros_like(value[:1])
            if ahead:
                return jnp.concatenate([value[1:], none], axis=0) - value
            return value - jnp.concatenate([none, value[:-1]], axis=0)
        length = value.shape[axis]
        spots = row3 if axis == 1 else lane3
        if ahead:
            return jnp.where(spots == length - 1, 0.0, pltpu.roll(value, length - 1, axis)) - value
        return value - jnp.where(spots == 0, 0.0, pltpu.roll(value, 1, axis))

    def edge_y(window, k):
        other = got_y[window, k][None]
        none = jnp.zeros((size_y - 1, size_z, LANES), F32)
        return jnp.concatenate([none, other] if window % 2 == 0 else [other, none], axis=0)

    def edge_z(window, k):
        return jnp.where(row3 == (size_z - 1 if window % 2 == 0 else 0), got_z[window, k], 0.0)

    def edge_x(window, k):
        landed = got_x[window]
        edges = []
        for y in range(size_y):
            spot = k * size_y + y
            amount = (LANES - 1 - spot) if window % 2 == 0 else (LANES - spot) % LANES
            edges.append(pltpu.roll(landed, amount, 1) if amount else landed)
        return jnp.where(lane3 == (size_x - 1 if window % 2 == 0 else 0), jnp.stack(edges, axis=0), 0.0)

    ex, ey, ez = fields[0], fields[1], fields[2]
    start_halo(0, (ez, ex), (ey, ex), (ez, ey))
    loading[1].wait()
    rate = COURANT / permit[...]
    loading[2].wait()
    hx, hy, hz = fields[3], fields[4], fields[5]
    spec_from = spectra
    for n in range(STEPS):
        window = 2 * n
        hx = hx - COURANT * (inner(True, 0, ez) - inner(True, 1, ey))
        hy = hy - COURANT * (inner(True, 1, ex) - inner(True, 2, ez))
        hz = hz - COURANT * (inner(True, 2, ey) - inner(True, 0, ex))
        tables_of(window)
        wait_halo(window)
        hx = hx - COURANT * (edge_y(window, 0) - edge_z(window, 0))
        hy = hy - COURANT * (edge_z(window, 1) - edge_x(window, 0))
        hz = hz - COURANT * (edge_x(window, 1) - edge_y(window, 1))
        window = 2 * n + 1
        start_halo(window, (hz, hx), (hy, hx), (hz, hy))
        half_c, half_s = run_c[2 * n : 2 * n + 1, :], run_s[2 * n : 2 * n + 1, :]
        for c, value in enumerate((hx, hy, hz)):
            spectra_out[3 + c] = spec_from[3 + c] + value * half_c
            spectra_out[9 + c] = spec_from[9 + c] - value * half_s
        ex = ex + rate * (inner(False, 0, hz) - inner(False, 1, hy))
        ey = ey + rate * (inner(False, 1, hx) - inner(False, 2, hz))
        ez = ez + rate * (inner(False, 2, hy) - inner(False, 0, hx))
        tables_of(window)
        wait_halo(window)
        ex = ex - rate * (edge_y(window, 0) - edge_z(window, 0))
        ey = ey - rate * (edge_z(window, 1) - edge_x(window, 0))
        ez = ez - rate * (edge_x(window, 1) - edge_y(window, 1))
        if n < STEPS - 1:
            start_halo(window + 1, (ez, ex), (ey, ex), (ez, ey))
        full_c, full_s = run_c[2 * n + 1 : 2 * n + 2, :], run_s[2 * n + 1 : 2 * n + 2, :]
        for c, value in enumerate((ex, ey, ez)):
            spectra_out[c] = spec_from[c] + value * full_c
            spectra_out[6 + c] = spec_from[6 + c] - value * full_s
        spec_from = spectra_out
    for c, value in enumerate((ex, ey, ez, hx, hy, hz)):
        fields_out[c] = value

    own_walls = walls.at[gz]
    lane_block = iota((8, LANES), 1) // PATCH
    sub = iota((8, LANES), 0)
    own_block = lane_block == sub
    z_row = iota((size_z, LANES), 0)
    own_walls[...] = jnp.zeros((8, LANES), F32)
    for y in range(size_y):
        spread = jnp.zeros((size_z, LANES), F32)
        for c in range(8):
            k = c % 4
            from_c = X_PICKS[k] + (6 if c >= 4 else 0)
            column = jnp.sum(jnp.where(lane == x_wall, spectra_out[from_c, y], 0.0), axis=1, keepdims=True)
            spread = jnp.where(lane == c * PATCH + z_row, column * (CURRENT_SIGNS[k] * facing_x), spread)
        record = jnp.sum(spread, axis=0, keepdims=True)
        own_walls[pl.ds(y, 1), :] = record
        for c in range(8):
            k = c % 4
            from_c = Z_PICKS[k] + (6 if c >= 4 else 0)
            low = spectra_out[from_c, y, pl.ds(ZB, 1), :]
            high = spectra_out[from_c, y, pl.ds(size_z - 1 - ZB, 1), :]
            picked = jnp.where(gz == 0, low, high) * (CURRENT_SIGNS[k] * facing_z * end_weight)
            cap_plane[pl.ds(8 * y + c, 1), :] = picked
        wall_hi, wall_lo = split(jnp.where(own_block, record, 0.0) * norm)
        cap_hi, cap_lo = split(cap_plane[pl.ds(8 * y, 8), :] * norm)
        none = jnp.zeros((8, LANES), BF16)
        for at, (cap_part, wall_part) in enumerate(((cap_hi, wall_hi), (cap_lo, wall_lo))):
            first = at * all_rows + 8 * y
            lhs[pl.ds(first, 8), :] = jnp.concatenate([cap_part, none], axis=1)
            lhs[pl.ds(first + half_rows, 8), :] = jnp.concatenate([none, wall_part], axis=1)

    lanes8 = iota((1, LANES), 1)
    owner_row = jnp.zeros((1, LANES), F32)
    for p in range(size_y):
        owner_row = jnp.where(lanes8 == 8 * gz + p, (wall_owner[0, p] + 1).astype(F32), owner_row)
    own_walls[pl.ds(size_y, 1), :] = owner_row

    def wall_copy(k):
        return pltpu.make_async_remote_copy(
            src_ref=walls.at[gz],
            dst_ref=walls.at[gz],
            send_sem=wall_send.at[k],
            recv_sem=wall_got.at[gz],
            device_id={"gz": (gz + k) % slabs},
            device_id_type=MESH,
        )

    def wall_landing(s):
        return pltpu.make_async_remote_copy(
            src_ref=walls.at[s], dst_ref=walls.at[s], send_sem=wall_send.at[0], recv_sem=wall_got.at[s],
            device_id={"gz": (gz + 1) % slabs}, device_id_type=MESH,
        )

    def cap_copy(k, at):
        return pltpu.make_async_remote_copy(
            src_ref=caps.at[at],
            dst_ref=caps.at[at],
            send_sem=cap_send.at[k],
            recv_sem=cap_got.at[at],
            device_id={"gz": (gz + k) % slabs},
            device_id_type=MESH,
        )

    for k in range(1, slabs):
        wall_copy(k).start()
    for at, holder in enumerate((0, slabs - 1)):
        @pl.when(gz == holder)
        def _():
            for y in range(size_y):
                caps[at, pl.ds(8 * y, 8), :] = block_transpose(cap_plane[pl.ds(8 * y, 8), :])
            for k in range(1, slabs):
                cap_copy(k, at).start()

    sign = jnp.where(sub < 4, -1.0, 1.0)

    def far_of(j):
        rows = lhs[...]
        by_high = jnp.dot(rows, table_hi[j], preferred_element_type=F32)
        by_low = jnp.dot(rows[:all_rows], table_lo[j], preferred_element_type=F32)
        product = by_high[:all_rows] + by_high[all_rows:] + by_low
        theta = jnp.zeros((8, LANES), F32)
        phi = jnp.zeros((8, LANES), F32)
        for face in range(2):
            sum_c = jnp.zeros((8, LANES), F32)
            sum_s = jnp.zeros((8, LANES), F32)
            for y in range(size_y):
                g = face * size_y + y
                tile = product[8 * g : 8 * g + 8]
                tile = tile[:, :LANES] + sign * pltpu.roll(tile[:, LANES:], 4, 0)
                sum_c = sum_c + tile * phases[j, 0, pl.ds(g, 1), :]
                sum_s = sum_s + tile * phases[j, 1, pl.ds(g, 1), :]
            far = sum_c + sign * pltpu.roll(sum_s, 4, 0)
            theta = theta + weights[j, 2 * face] * far
            phi = phi + weights[j, 2 * face + 1] * far

        def four(values):
            pairs = values + pltpu.roll(values, 7, 0)
            return pairs + pltpu.roll(pairs, 6, 0)

        parts_out[j] = jnp.where(sub % 4 == 1, pltpu.roll(four(phi), 1, 0), four(theta))

    chunk = me // ratio

    bunch = 4 if chunks % 4 == 0 else 1

    def partner(number):
        other, bit = 0, 1
        while bit < chunks:
            other = other + bit * ((chunk // bit + number // bit) % 2)
            bit *= 2
        return other

    def part_copy(k):
        peer = (me + k) % peers
        return pltpu.make_async_remote_copy(
            src_ref=parts_out.at[peer // ratio],
            dst_ref=parts_in.at[k],
            send_sem=part_send.at[k],
            recv_sem=part_got.at[k],
            device_id=ident(peer),
            device_id_type=MESH,
        )

    def each_peer(act):
        def body(k, carry):
            act(k)
            return carry

        lax.fori_loop(1, peers, body, 0)

    def far_and_send(number, carry):
        several = [partner(chunks - 1 - bunch * number - m) for m in range(bunch)]
        for to in several:
            far_of(to)

        def send(m, inner_carry):
            to = partner(chunks - 1 - bunch * number - m // ratio)
            peer = to * ratio + m % ratio

            @pl.when(peer != me)
            def _():
                part_copy((peer - me + peers) % peers).start()

            return inner_carry

        lax.fori_loop(0, bunch * ratio, send, 0)
        return carry

    lax.fori_loop(0, chunks // bunch, far_and_send, 0)
    parts_in[0] = parts_out[chunk]

    for s in range(slabs):
        @pl.when(s != gz)
        def _():
            wall_landing(s).wait_recv()
    for at, holder in enumerate((0, slabs - 1)):
        @pl.when(gz != holder)
        def _():
            cap_copy(1, at).wait_recv()

    def choose(mine, share, records):
        length = mine.shape[1]
        before = jnp.where(iota((length, length), 0) < iota((length, length), 1), 1.0, 0.0).astype(BF16)
        ones = jnp.broadcast_to(jnp.where(mine, 1.0, 0.0), (8, length))
        rank = jnp.dot(ones.astype(BF16), before, preferred_element_type=F32)
        wanted = iota((8, length), 0).astype(F32)
        chooser = jnp.where(rank == wanted, ones, 0.0)
        return jnp.dot(chooser, records, precision=HIGHEST, preferred_element_type=F32)[:share]

    all_walls = walls[...]
    owner_all = jnp.sum(all_walls[:, size_y : size_y + 1, :], axis=0)[:, : 8 * slabs]
    cap_share = (owned_out.shape[0] - size_y) // 2
    owned_out[pl.ds(0, size_y), 0, :] = choose(
        owner_all == (gz + 1).astype(F32), size_y, all_walls.reshape(8 * slabs, LANES)
    )
    for at in range(2):
        owned_out[pl.ds(size_y + at * cap_share, cap_share), 0, :] = choose(
            cap_owner[pl.ds(at, 1), :] == gz, cap_share, caps[at]
        )

    each_peer(lambda k: part_copy(k).wait_recv())
    field = jnp.sum(parts_in[...], axis=0)
    power = jnp.where(sub % 4 < 2, field * field, 0.0)
    intensity = jnp.sum(power, axis=0, keepdims=True)
    intensity_out[...] = intensity
    residual = aim[pl.ds(chunk, 1), :].astype(F32) * (intensity - target[pl.ds(chunk, 1), :])
    leads = me % ratio == 0

    def slope_copy(k, of):
        return pltpu.make_async_remote_copy(
            src_ref=slopes.at[of],
            dst_ref=slopes.at[of],
            send_sem=slope_send.at[k],
            recv_sem=slope_got.at[of],
            device_id=ident((me + k) % peers),
            device_id_type=MESH,
        )

    @pl.when(leads)
    def _():
        slopes[chunk] = 2.0 * residual * field
        each_peer(lambda k: slope_copy(k, chunk).start())

    def adjoint_of(j):
        slope = slopes[j]
        by_theta = jnp.where(sub < 4, slope[0:1], slope[4:5])
        by_phi = jnp.where(sub < 4, slope[1:2], slope[5:6])
        tiles = []
        for face in range(2):
            vector = weights[j, 2 * face] * by_theta + weights[j, 2 * face + 1] * by_phi
            turned = -sign * pltpu.roll(vector, 4, 0)
            for y in range(size_y):
                g = face * size_y + y
                tile = vector * phases[j, 0, pl.ds(g, 1), :] + turned * phases[j, 1, pl.ds(g, 1), :]
                tiles.append(jnp.concatenate([tile, -sign * pltpu.roll(tile, 4, 0)], axis=1))
        rows = jnp.concatenate(tiles, axis=0)
        high, low = split(rows)
        both = jnp.concatenate([high, low], axis=0)
        across = (((1,), (1,)), ((), ()))
        by_high = lax.dot_general(both, table_hi[j], across, preferred_element_type=F32)
        by_low = lax.dot_general(high, table_lo[j], across, preferred_element_type=F32)
        return by_high[:all_rows] + by_high[all_rows:] + by_low

    def adjoint_some(number, total):
        several = [partner(bunch * number + m) for m in range(bunch)]
        for j in several:
            @pl.when(j * ratio != me)
            def _():
                slope_copy(1, j).wait_recv()

        for j in several:
            total = total + adjoint_of(j)
        return total

    gradient = lax.fori_loop(0, chunks // bunch, adjoint_some, jnp.zeros((all_rows, size_x + 8 * size_z), F32))
    for y in range(size_y):
        wall = gradient[half_rows + 8 * y : half_rows + 8 * y + 8, size_x:]
        adjoint_out[pl.ds(y, 1), 0, :] = jnp.sum(jnp.where(own_block, wall, 0.0), axis=0, keepdims=True) * norm
        cap = block_transpose(gradient[8 * y : 8 * y + 8, :size_x] * (norm * end_weight))
        adjoint_out[pl.ds(size_y + 8 * y, 8), 0, :] = cap

    for window in range(windows):
        for copy, sends, receives in halo_copies(window):
            @pl.when(sends)
            def _():
                copy.wait_send()
    each_peer(lambda k: part_copy(k).wait_send())

    @pl.when(leads)
    def _():
        each_peer(lambda k: slope_copy(k, chunk).wait_send())

    for k in range(1, slabs):
        wall_copy(k).wait_send()
    for at, holder in enumerate((0, slabs - 1)):
        @pl.when(gz == holder)
        def _():
            for k in range(1, slabs):
                cap_copy(k, at).wait_send()


def write_out(*refs):
    copies = [pltpu.make_async_copy(refs[i], refs[5 + i], refs[10].at[i]) for i in range(5)]
    for copy in copies:
        copy.start()
    for copy in copies:
        copy.wait()


def local(fields, spectra, permittivity, phase_start, wall_owner, cap_owner, dir_index, target, aim_mask):
    slabs, devs, xys = (lax.axis_size(a) for a in ("gz", "dev", "xy"))
    peers = slabs * devs * xys
    size_y, size_z, size_x = permittivity.shape
    assert size_z == PATCH and size_x == LANES and size_y == 4
    directions = dir_index.shape[0]
    chunks = directions // LANES
    ratio = peers // chunks
    share = directions // peers
    cap_count = size_y * size_x // PATCH
    owned = size_y + 2 * (cap_count // slabs)
    rows = 16 * size_y
    depth = size_x + 8 * size_z
    windows = 2 * STEPS
    vmem, smem = (pl.BlockSpec(memory_space=s) for s in (pltpu.VMEM, pltpu.SMEM))
    anywhere = pl.BlockSpec(memory_space=pl.ANY)
    dma = pltpu.SemaphoreType.DMA
    outs = pl.pallas_call(
        functools.partial(kernel, (slabs, devs, xys)),
        out_shape=(
            pltpu.VMEM(fields.shape, F32),
            pltpu.VMEM(spectra.shape, F32),
            pltpu.VMEM((owned, 1, LANES), F32),
            pltpu.VMEM((1, LANES), F32),
            pltpu.VMEM((size_y + cap_count, 1, LANES), F32),
        ),
        in_specs=[anywhere, anywhere, anywhere, vmem, smem, vmem, vmem, vmem, vmem],
        out_specs=(vmem,) * 5,
        scratch_shapes=[
            pltpu.VMEM((windows, 2, size_z, LANES), F32),
            pltpu.VMEM((windows, 2, size_y, 1, LANES), F32),
            pltpu.VMEM((windows, size_z, LANES), F32),
            pltpu.VMEM((windows, 2, size_z, LANES), F32),
            pltpu.VMEM((windows, 2, size_y, 1, LANES), F32),
            pltpu.VMEM((windows, size_z, LANES), F32),
            pltpu.VMEM(fields.shape, F32),
            pltpu.VMEM(spectra.shape, F32),
            pltpu.VMEM(permittivity.shape, F32),
            pltpu.VMEM((8, chunks, LANES), F32),
            pltpu.VMEM((chunks, 4, 8, LANES), F32),
            pltpu.VMEM((chunks, 2, 2 * size_y, LANES), F32),
            pltpu.VMEM((chunks, depth, 2 * LANES), BF16),
            pltpu.VMEM((chunks, depth, 2 * LANES), BF16),
            pltpu.VMEM((8 * size_y, LANES), F32),
            pltpu.VMEM((2 * rows, depth), BF16),
            pltpu.VMEM((chunks, 8, LANES), F32),
            pltpu.VMEM((peers, 8, LANES), F32),
            pltpu.VMEM((chunks, 8, LANES), F32),
            pltpu.VMEM((slabs, 8, LANES), F32),
            pltpu.VMEM((2, cap_count, LANES), F32),
            dma((windows, 3)), dma((windows, 3)),
            dma((peers,)), dma((peers,)),
            dma((peers,)), dma((chunks,)),
            dma((slabs,)), dma((slabs,)),
            dma((slabs,)), dma((2,)),
            dma((3,)),
        ],
        compiler_params=pltpu.CompilerParams(collective_id=0, has_side_effects=True),
    )(
        fields, spectra, permittivity, phase_start.reshape(1, 1), wall_owner, cap_owner,
        dir_index.reshape(chunks, LANES), target.reshape(chunks, LANES), aim_mask.reshape(chunks, LANES),
    )
    held = (fields.shape, spectra.shape, (owned, 1, LANES), (1, LANES), (size_y + cap_count, 1, LANES))
    fields_new, spectra_new, owned_rows, intensity, adjoint = pl.pallas_call(
        write_out,
        out_shape=tuple(jax.ShapeDtypeStruct(shape, F32) for shape in held),
        in_specs=[pl.BlockSpec(memory_space=pltpu.VMEM)] * 5,
        out_specs=(pl.BlockSpec(memory_space=pl.ANY),) * 5,
        scratch_shapes=[dma((5,))],
    )(*(pltpu.with_memory_space_constraint(out, pltpu.VMEM) for out in outs))
    owned_rows = owned_rows.reshape(1, 1, owned, 1, LANES).transpose(0, 1, 3, 2, 4)
    adjoint = adjoint.reshape(1, 1, size_y + cap_count, 1, LANES).transpose(0, 1, 3, 2, 4)
    intensity = intensity.reshape(LANES)
    if ratio > 1:
        me = (lax.axis_index("gz") * devs + lax.axis_index("dev")) * xys + lax.axis_index("xy")
        intensity = lax.dynamic_slice_in_dim(intensity, (me % ratio) * share, share, 0)
    return (fields_new, spectra_new, owned_rows, intensity, adjoint)


def solution(mesh):
    placed = (
        P("groups", "dev", "gz", "xy"),
        P("groups", "dev", "gz", "xy"),
        P(("groups", "dev"), "gz", "xy"),
        P("groups"),
        P("gz", None),
        P(),
        P(),
        P("groups"),
        P("groups"),
    )
    return jax.shard_map(
        local,
        mesh=mesh,
        in_specs=placed,
        out_specs=(
            P("groups", "dev", "gz", "xy"),
            P("groups", "dev", "gz", "xy"),
            P(("groups", "gz"), "dev", "xy", None, None),
            P(("groups", "gz", "dev", "xy")),
            P(("groups", "gz"), "dev", "xy", None, None),
        ),
        check_vma=False,
    )
```

```python
import functools
import math

import jax
import jax.numpy as jnp
from jax import lax
from jax.experimental import pallas as pl
from jax.experimental.pallas import tpu as pltpu
from jax.sharding import PartitionSpec as P

PATCH = 16
XB = 8
ZB = 4
STEPS = 3
THETAS = 64
COURANT = 0.5
ANGULAR_STEP = 0.3
WAVE_NUMBER = 0.6
LANES = 128
HIGHEST = lax.Precision.HIGHEST
CURRENT_SIGNS = (-1.0, 1.0, 1.0, -1.0)
X_PICKS = (5, 4, 2, 1)
Z_PICKS = (4, 3, 1, 0)
MESH = pl.DeviceIdType.MESH
AXES = ("dev", "gz", "xy")
F32 = jnp.float32
BF16 = jnp.bfloat16


def iota(shape, dim):
    return lax.broadcasted_iota(jnp.int32, shape, dim)


def sincos(turns):
    half = (turns - jnp.floor(turns + 0.5)) * math.pi
    sq = half * half
    sin_h = half * (1.0 + sq * (-1.0 / 6 + sq * (1.0 / 120 + sq * (-1.0 / 5040 + sq * (1.0 / 362880 - sq * (1.0 / 39916800))))))
    cos_h = 1.0 + sq * (-0.5 + sq * (1.0 / 24 + sq * (-1.0 / 720 + sq * (1.0 / 40320 + sq * (-1.0 / 3628800 + sq * (1.0 / 479001600))))))
    return 2.0 * sin_h * cos_h, 1.0 - 2.0 * sin_h * sin_h


def split(values):
    high = values.astype(BF16)
    return high, (values - high.astype(F32)).astype(BF16)


def block_transpose(tile):
    on_diagonal = (iota(tile.shape, 1) // PATCH) == iota(tile.shape, 0)
    total = jnp.where(on_diagonal, tile, 0.0)
    for k in range(1, 8):
        turned = pltpu.roll(tile, PATCH * k, 1)
        total = total + pltpu.roll(jnp.where(on_diagonal, turned, 0.0), 8 - k, 0)
    return total


def kernel(
    sizes,
    fields_in, spectra_in, permit_in, phase, wall_owner, cap_owner, dirs, target, aim,
    fields_out, spectra_out, owned_out, intensity_out, adjoint_out,
    send_y, send_z, send_x, got_y, got_z, got_x,
    fields, spectra, permit, geo, weights, phases, table_hi, table_lo, cap_plane, lhs,
    parts_out, parts_in, slopes, walls, caps,
    halo_send, halo_got, part_send, part_got, slope_send, slope_got, wall_send, wall_got, cap_send, cap_got, loads,
):
    slabs, devs, xys = sizes
    peers = slabs * devs * xys
    size_y, size_z, size_x = permit.shape
    chunks = dirs.shape[0]
    ratio = peers // chunks
    groups = 2 * size_y
    half_rows = 8 * size_y
    all_rows = 2 * half_rows
    gz, dev, xy = lax.axis_index("gz"), lax.axis_index("dev"), lax.axis_index("xy")
    me = (gz * devs + dev) * xys + xy
    place = {"dev": dev, "gz": gz, "xy": xy}
    count = {"dev": devs, "gz": slabs, "xy": xys}

    loading = [
        pltpu.make_async_copy(source, held, loads.at[number])
        for number, (source, held) in enumerate(((fields_in, fields), (permit_in, permit), (spectra_in, spectra)))
    ]
    for copy in loading:
        copy.start()

    def ident(flat):
        return {"gz": flat // (devs * xys), "dev": (flat // xys) % devs, "xy": flat % xys}

    barrier = pltpu.get_barrier_semaphore()

    def greet(k, carry):
        pl.semaphore_signal(barrier, inc=1, device_id=ident((me + k) % peers), device_id_type=MESH)
        return carry

    lax.fori_loop(1, peers, greet, 0)

    index = dirs[...]
    sin_t, cos_t = sincos(((index // THETAS).astype(F32) + 0.5) * (0.5 / THETAS))
    sin_f, cos_f = sincos((index % THETAS).astype(F32) * (1.0 / THETAS))
    wave = WAVE_NUMBER / (2.0 * math.pi)
    for slot, values in enumerate((
        wave * sin_t * cos_f, wave * sin_t * sin_f, wave * cos_t,
        cos_t * cos_f, cos_t * sin_f, -sin_t, -sin_f, cos_f,
    )):
        geo[slot] = values

    grid_x, grid_y, grid_z = size_x * xys, size_y * devs, size_z * slabs
    x_first = (xy * size_x).astype(F32) - (grid_x - 1) / 2.0
    y_first = (dev * size_y).astype(F32) - (grid_y - 1) / 2.0
    z_first = (gz * size_z).astype(F32) - (grid_z - 1) / 2.0
    x_wall = jnp.where(xy == 0, XB, size_x - 1 - XB)
    z_cap = jnp.where(gz == 0, ZB, size_z - 1 - ZB)
    x_face = x_first + x_wall.astype(F32)
    z_face = z_first + z_cap.astype(F32)
    facing_x = jnp.where(xy == 0, -1.0, 1.0)
    facing_z = jnp.where(gz == 0, -1.0, 1.0)
    is_end = jnp.logical_or(gz == 0, gz == slabs - 1)
    end_weight = jnp.where(is_end, 1.0, 0.0)
    norm = 1.0 / math.sqrt(2.0 * (2 * grid_y * grid_z + 2 * grid_y * grid_x))

    def make_tables(j, carry):
        def row(slot):
            return geo[slot, pl.ds(j, 1), :]

        ux, uy, uz = row(0), row(1), row(2)
        blocks = size_x // 8
        far_s, far_c = sincos((iota((blocks, LANES), 0).astype(F32) * 8.0 + x_first) * ux)
        near_s, near_c = sincos(iota((8, LANES), 0).astype(F32) * ux)
        far_s, far_c = far_s[:, None, :], far_c[:, None, :]
        near_s, near_c = near_s[None], near_c[None]
        cos_x = (far_c * near_c - far_s * near_s).reshape(size_x, LANES)
        sin_x = (far_s * near_c + far_c * near_s).reshape(size_x, LANES)
        sin_z, cos_z = sincos((iota((size_z, LANES), 0).astype(F32) + z_first) * uz)
        for at, (x_part, z_part) in enumerate(((cos_x, cos_z), (sin_x, sin_z))):
            lanes = pl.ds(at * LANES, LANES)
            x_high, x_low = split(x_part)
            z_high, z_low = split(z_part)
            table_hi[j, pl.ds(0, size_x), lanes] = x_high
            table_lo[j, pl.ds(0, size_x), lanes] = x_low
            table_hi[j, pl.ds(size_x, 8 * size_z), lanes] = jnp.concatenate([z_high] * 8, axis=0)
            table_lo[j, pl.ds(size_x, 8 * size_z), lanes] = jnp.concatenate([z_low] * 8, axis=0)
        which = iota((groups, LANES), 0)
        cell_y = (which % size_y).astype(F32) + y_first
        sin_g, cos_g = sincos(cell_y * uy + jnp.where(which < size_y, z_face * uz, x_face * ux))
        phases[j, 0] = cos_g
        phases[j, 1] = sin_g
        kind = iota((8, LANES), 0) % 4

        def pattern(a, b, c, d):
            return jnp.where(kind == 0, a, jnp.where(kind == 1, b, jnp.where(kind == 2, c, d)))

        tx, ty, tz, fx, fy = row(3), row(4), row(5), row(6), row(7)
        weights[j, 0] = pattern(-tx, -ty, -fx, -fy)
        weights[j, 1] = pattern(-fx, -fy, tx, ty)
        weights[j, 2] = pattern(-ty, -tz, -fy, jnp.zeros_like(fy))
        weights[j, 3] = pattern(-fy, jnp.zeros_like(fy), ty, tz)
        return carry

    windows = 2 * STEPS

    def tables_of(window):
        lax.fori_loop(window * chunks // windows, (window + 1) * chunks // windows, make_tables, 0)

    order = iota((8, LANES), 0).astype(F32)
    run_s, run_c = sincos((phase[...] + 0.5 * ANGULAR_STEP * (order + 1.0)) * (0.5 / math.pi))

    for number, (axis, got) in enumerate(zip(AXES, (got_y, got_z, got_x))):
        @pl.when(place[axis] == count[axis] - 1)
        def _():
            for window in range(0, windows, 2):
                got[window] = jnp.zeros(got.shape[1:], F32)

        @pl.when(place[axis] == 0)
        def _():
            for window in range(1, windows, 2):
                got[window] = jnp.zeros(got.shape[1:], F32)

    loading[0].wait()
    pl.semaphore_wait(barrier, peers - 1)

    lane = iota((size_z, LANES), 1)
    lane3 = iota((size_y, size_z, LANES), 2)
    row3 = iota((size_y, size_z, LANES), 1)

    def halo_copies(window):
        step = -1 if window % 2 == 0 else 1
        copies = []
        for number, (axis, source, landing) in enumerate(
            zip(AXES, (send_y, send_z, send_x), (got_y, got_z, got_x))
        ):
            mine, total = place[axis], count[axis]
            copy = pltpu.make_async_remote_copy(
                src_ref=source.at[window],
                dst_ref=landing.at[window],
                send_sem=halo_send.at[window, number],
                recv_sem=halo_got.at[window, number],
                device_id={axis: (mine + step + total) % total},
                device_id_type=MESH,
            )
            if step < 0:
                copies.append((copy, mine > 0, mine < total - 1))
            else:
                copies.append((copy, mine < total - 1, mine > 0))
        return copies

    def start_halo(window, for_y, for_z, for_x):
        ahead = window % 2 == 0
        at_y, at_z = (0, 0) if ahead else (size_y - 1, size_z - 1)
        for k in range(2):
            send_y[window, k] = for_y[k][at_y]
            send_z[window, k] = for_z[k][:, at_z : at_z + 1, :]
        copies = halo_copies(window)
        for copy, sends, receives in copies[:2]:
            @pl.when(sends)
            def _():
                copy.start()
        packed = jnp.zeros((size_z, LANES), F32)
        for k in range(2):
            for y in range(size_y):
                spot = k * size_y + y
                amount = spot if ahead else (spot + 1) % LANES
                value = for_x[k][y]
                turned = pltpu.roll(value, amount, 1) if amount else value
                packed = jnp.where(lane == spot, turned, packed)
        send_x[window] = packed
        copy, sends, receives = copies[2]

        @pl.when(sends)
        def _():
            copy.start()

    def wait_halo(window):
        for copy, sends, receives in halo_copies(window):
            @pl.when(receives)
            def _():
                copy.wait_recv()

    def inner(ahead, axis, value):
        if axis == 0:
            none = jnp.zeros_like(value[:1])
            if ahead:
                return jnp.concatenate([value[1:], none], axis=0) - value
            return value - jnp.concatenate([none, value[:-1]], axis=0)
        length = value.shape[axis]
        spots = row3 if axis == 1 else lane3
        if ahead:
            return jnp.where(spots == length - 1, 0.0, pltpu.roll(value, length - 1, axis)) - value
        return value - jnp.where(spots == 0, 0.0, pltpu.roll(value, 1, axis))

    def edge_y(window, k):
        other = got_y[window, k][None]
        none = jnp.zeros((size_y - 1, size_z, LANES), F32)
        return jnp.concatenate([none, other] if window % 2 == 0 else [other, none], axis=0)

    def edge_z(window, k):
        return jnp.where(row3 == (size_z - 1 if window % 2 == 0 else 0), got_z[window, k], 0.0)

    def edge_x(window, k):
        landed = got_x[window]
        edges = []
        for y in range(size_y):
            spot = k * size_y + y
            amount = (LANES - 1 - spot) if window % 2 == 0 else (LANES - spot) % LANES
            edges.append(pltpu.roll(landed, amount, 1) if amount else landed)
        return jnp.where(lane3 == (size_x - 1 if window % 2 == 0 else 0), jnp.stack(edges, axis=0), 0.0)

    ex, ey, ez = fields[0], fields[1], fields[2]
    start_halo(0, (ez, ex), (ey, ex), (ez, ey))
    loading[1].wait()
    rate = COURANT / permit[...]
    loading[2].wait()
    hx, hy, hz = fields[3], fields[4], fields[5]
    spec_from = spectra
    for n in range(STEPS):
        window = 2 * n
        hx = hx - COURANT * (inner(True, 0, ez) - inner(True, 1, ey))
        hy = hy - COURANT * (inner(True, 1, ex) - inner(True, 2, ez))
        hz = hz - COURANT * (inner(True, 2, ey) - inner(True, 0, ex))
        tables_of(window)
        wait_halo(window)
        hx = hx - COURANT * (edge_y(window, 0) - edge_z(window, 0))
        hy = hy - COURANT * (edge_z(window, 1) - edge_x(window, 0))
        hz = hz - COURANT * (edge_x(window, 1) - edge_y(window, 1))
        window = 2 * n + 1
        start_halo(window, (hz, hx), (hy, hx), (hz, hy))
        half_c, half_s = run_c[2 * n : 2 * n + 1, :], run_s[2 * n : 2 * n + 1, :]
        for c, value in enumerate((hx, hy, hz)):
            spectra_out[3 + c] = spec_from[3 + c] + value * half_c
            spectra_out[9 + c] = spec_from[9 + c] - value * half_s
        ex = ex + rate * (inner(False, 0, hz) - inner(False, 1, hy))
        ey = ey + rate * (inner(False, 1, hx) - inner(False, 2, hz))
        ez = ez + rate * (inner(False, 2, hy) - inner(False, 0, hx))
        tables_of(window)
        wait_halo(window)
        ex = ex - rate * (edge_y(window, 0) - edge_z(window, 0))
        ey = ey - rate * (edge_z(window, 1) - edge_x(window, 0))
        ez = ez - rate * (edge_x(window, 1) - edge_y(window, 1))
        if n < STEPS - 1:
            start_halo(window + 1, (ez, ex), (ey, ex), (ez, ey))
        full_c, full_s = run_c[2 * n + 1 : 2 * n + 2, :], run_s[2 * n + 1 : 2 * n + 2, :]
        for c, value in enumerate((ex, ey, ez)):
            spectra_out[c] = spec_from[c] + value * full_c
            spectra_out[6 + c] = spec_from[6 + c] - value * full_s
        spec_from = spectra_out
    for c, value in enumerate((ex, ey, ez, hx, hy, hz)):
        fields_out[c] = value

    own_walls = walls.at[gz]
    lane_block = iota((8, LANES), 1) // PATCH
    sub = iota((8, LANES), 0)
    own_block = lane_block == sub
    z_row = iota((size_z, LANES), 0)
    own_walls[...] = jnp.zeros((8, LANES), F32)
    for y in range(size_y):
        spread = jnp.zeros((size_z, LANES), F32)
        for c in range(8):
            k = c % 4
            from_c = X_PICKS[k] + (6 if c >= 4 else 0)
            column = jnp.sum(jnp.where(lane == x_wall, spectra_out[from_c, y], 0.0), axis=1, keepdims=True)
            spread = jnp.where(lane == c * PATCH + z_row, column * (CURRENT_SIGNS[k] * facing_x), spread)
        record = jnp.sum(spread, axis=0, keepdims=True)
        own_walls[pl.ds(y, 1), :] = record
        for c in range(8):
            k = c % 4
            from_c = Z_PICKS[k] + (6 if c >= 4 else 0)
            low = spectra_out[from_c, y, pl.ds(ZB, 1), :]
            high = spectra_out[from_c, y, pl.ds(size_z - 1 - ZB, 1), :]
            picked = jnp.where(gz == 0, low, high) * (CURRENT_SIGNS[k] * facing_z * end_weight)
            cap_plane[pl.ds(8 * y + c, 1), :] = picked
        wall_hi, wall_lo = split(jnp.where(own_block, record, 0.0) * norm)
        cap_hi, cap_lo = split(cap_plane[pl.ds(8 * y, 8), :] * norm)
        none = jnp.zeros((8, LANES), BF16)
        for at, (cap_part, wall_part) in enumerate(((cap_hi, wall_hi), (cap_lo, wall_lo))):
            first = at * all_rows + 8 * y
            lhs[pl.ds(first, 8), :] = jnp.concatenate([cap_part, none], axis=1)
            lhs[pl.ds(first + half_rows, 8), :] = jnp.concatenate([none, wall_part], axis=1)

    lanes8 = iota((1, LANES), 1)
    owner_row = jnp.zeros((1, LANES), F32)
    for p in range(size_y):
        owner_row = jnp.where(lanes8 == 8 * gz + p, (wall_owner[0, p] + 1).astype(F32), owner_row)
    own_walls[pl.ds(size_y, 1), :] = owner_row

    def wall_copy(k):
        return pltpu.make_async_remote_copy(
            src_ref=walls.at[gz],
            dst_ref=walls.at[gz],
            send_sem=wall_send.at[k],
            recv_sem=wall_got.at[gz],
            device_id={"gz": (gz + k) % slabs},
            device_id_type=MESH,
        )

    def wall_landing(s):
        return pltpu.make_async_remote_copy(
            src_ref=walls.at[s], dst_ref=walls.at[s], send_sem=wall_send.at[0], recv_sem=wall_got.at[s],
            device_id={"gz": (gz + 1) % slabs}, device_id_type=MESH,
        )

    def cap_copy(k, at):
        return pltpu.make_async_remote_copy(
            src_ref=caps.at[at],
            dst_ref=caps.at[at],
            send_sem=cap_send.at[k],
            recv_sem=cap_got.at[at],
            device_id={"gz": (gz + k) % slabs},
            device_id_type=MESH,
        )

    for k in range(1, slabs):
        wall_copy(k).start()
    for at, holder in enumerate((0, slabs - 1)):
        @pl.when(gz == holder)
        def _():
            for y in range(size_y):
                caps[at, pl.ds(8 * y, 8), :] = block_transpose(cap_plane[pl.ds(8 * y, 8), :])
            for k in range(1, slabs):
                cap_copy(k, at).start()

    sign = jnp.where(sub < 4, -1.0, 1.0)

    def far_of(j):
        rows = lhs[...]
        by_high = jnp.dot(rows, table_hi[j], preferred_element_type=F32)
        by_low = jnp.dot(rows[:all_rows], table_lo[j], preferred_element_type=F32)
        product = by_high[:all_rows] + by_high[all_rows:] + by_low
        theta = jnp.zeros((8, LANES), F32)
        phi = jnp.zeros((8, LANES), F32)
        for face in range(2):
            sum_c = jnp.zeros((8, LANES), F32)
            sum_s = jnp.zeros((8, LANES), F32)
            for y in range(size_y):
                g = face * size_y + y
                tile = product[8 * g : 8 * g + 8]
                tile = tile[:, :LANES] + sign * pltpu.roll(tile[:, LANES:], 4, 0)
                sum_c = sum_c + tile * phases[j, 0, pl.ds(g, 1), :]
                sum_s = sum_s + tile * phases[j, 1, pl.ds(g, 1), :]
            far = sum_c + sign * pltpu.roll(sum_s, 4, 0)
            theta = theta + weights[j, 2 * face] * far
            phi = phi + weights[j, 2 * face + 1] * far

        def four(values):
            pairs = values + pltpu.roll(values, 7, 0)
            return pairs + pltpu.roll(pairs, 6, 0)

        parts_out[j] = jnp.where(sub % 4 == 1, pltpu.roll(four(phi), 1, 0), four(theta))

    chunk = me // ratio

    bunch = 4 if chunks % 4 == 0 else 1

    def partner(number):
        other, bit = 0, 1
        while bit < chunks:
            other = other + bit * ((chunk // bit + number // bit) % 2)
            bit *= 2
        return other

    def part_copy(k):
        peer = (me + k) % peers
        return pltpu.make_async_remote_copy(
            src_ref=parts_out.at[peer // ratio],
            dst_ref=parts_in.at[k],
            send_sem=part_send.at[k],
            recv_sem=part_got.at[k],
            device_id=ident(peer),
            device_id_type=MESH,
        )

    def each_peer(act):
        def body(k, carry):
            act(k)
            return carry

        lax.fori_loop(1, peers, body, 0)

    def far_and_send(number, carry):
        several = [partner(chunks - 1 - bunch * number - m) for m in range(bunch)]
        for to in several:
            far_of(to)

        def send(m, inner_carry):
            to = partner(chunks - 1 - bunch * number - m // ratio)
            peer = to * ratio + m % ratio

            @pl.when(peer != me)
            def _():
                part_copy((peer - me + peers) % peers).start()

            return inner_carry

        lax.fori_loop(0, bunch * ratio, send, 0)
        return carry

    lax.fori_loop(0, chunks // bunch, far_and_send, 0)
    parts_in[0] = parts_out[chunk]

    for s in range(slabs):
        @pl.when(s != gz)
        def _():
            wall_landing(s).wait_recv()
    for at, holder in enumerate((0, slabs - 1)):
        @pl.when(gz != holder)
        def _():
            cap_copy(1, at).wait_recv()

    def choose(mine, share, records):
        length = mine.shape[1]
        before = jnp.where(iota((length, length), 0) < iota((length, length), 1), 1.0, 0.0).astype(BF16)
        ones = jnp.broadcast_to(jnp.where(mine, 1.0, 0.0), (8, length))
        rank = jnp.dot(ones.astype(BF16), before, preferred_element_type=F32)
        wanted = iota((8, length), 0).astype(F32)
        chooser = jnp.where(rank == wanted, ones, 0.0)
        return jnp.dot(chooser, records, precision=HIGHEST, preferred_element_type=F32)[:share]

    all_walls = walls[...]
    owner_all = jnp.sum(all_walls[:, size_y : size_y + 1, :], axis=0)[:, : 8 * slabs]
    cap_share = (owned_out.shape[0] - size_y) // 2
    owned_out[pl.ds(0, size_y), 0, :] = choose(
        owner_all == (gz + 1).astype(F32), size_y, all_walls.reshape(8 * slabs, LANES)
    )
    for at in range(2):
        owned_out[pl.ds(size_y + at * cap_share, cap_share), 0, :] = choose(
            cap_owner[pl.ds(at, 1), :] == gz, cap_share, caps[at]
        )

    each_peer(lambda k: part_copy(k).wait_recv())
    field = jnp.sum(parts_in[...], axis=0)
    power = jnp.where(sub % 4 < 2, field * field, 0.0)
    intensity = jnp.sum(power, axis=0, keepdims=True)
    intensity_out[...] = intensity
    residual = aim[pl.ds(chunk, 1), :].astype(F32) * (intensity - target[pl.ds(chunk, 1), :])
    leads = me % ratio == 0

    def slope_copy(k, of):
        return pltpu.make_async_remote_copy(
            src_ref=slopes.at[of],
            dst_ref=slopes.at[of],
            send_sem=slope_send.at[k],
            recv_sem=slope_got.at[of],
            device_id=ident((me + k) % peers),
            device_id_type=MESH,
        )

    @pl.when(leads)
    def _():
        slopes[chunk] = 2.0 * residual * field
        each_peer(lambda k: slope_copy(k, chunk).start())

    for window in range(windows):
        for copy, sends, receives in halo_copies(window):
            @pl.when(sends)
            def _():
                copy.wait_send()
    each_peer(lambda k: part_copy(k).wait_send())

    for k in range(1, slabs):
        wall_copy(k).wait_send()
    for at, holder in enumerate((0, slabs - 1)):
        @pl.when(gz == holder)
        def _():
            for k in range(1, slabs):
                cap_copy(k, at).wait_send()

    def adjoint_of(j):
        slope = slopes[j]
        by_theta = jnp.where(sub < 4, slope[0:1], slope[4:5])
        by_phi = jnp.where(sub < 4, slope[1:2], slope[5:6])
        tiles = []
        for face in range(2):
            vector = weights[j, 2 * face] * by_theta + weights[j, 2 * face + 1] * by_phi
            turned = -sign * pltpu.roll(vector, 4, 0)
            for y in range(size_y):
                g = face * size_y + y
                tile = vector * phases[j, 0, pl.ds(g, 1), :] + turned * phases[j, 1, pl.ds(g, 1), :]
                tiles.append(jnp.concatenate([tile, -sign * pltpu.roll(tile, 4, 0)], axis=1))
        rows = jnp.concatenate(tiles, axis=0)
        high, low = split(rows)
        both = jnp.concatenate([high, low], axis=0)
        across = (((1,), (1,)), ((), ()))
        by_high = lax.dot_general(both, table_hi[j], across, preferred_element_type=F32)
        by_low = lax.dot_general(high, table_lo[j], across, preferred_element_type=F32)
        return by_high[:all_rows] + by_high[all_rows:] + by_low

    def adjoint_some(number, total):
        several = [partner(bunch * number + m) for m in range(bunch)]
        for j in several:
            @pl.when(j * ratio != me)
            def _():
                slope_copy(1, j).wait_recv()

        for j in several:
            total = total + adjoint_of(j)
        return total

    gradient = lax.fori_loop(0, chunks // bunch, adjoint_some, jnp.zeros((all_rows, size_x + 8 * size_z), F32))
    for y in range(size_y):
        wall = gradient[half_rows + 8 * y : half_rows + 8 * y + 8, size_x:]
        adjoint_out[pl.ds(y, 1), 0, :] = jnp.sum(jnp.where(own_block, wall, 0.0), axis=0, keepdims=True) * norm
        cap = block_transpose(gradient[8 * y : 8 * y + 8, :size_x] * (norm * end_weight))
        adjoint_out[pl.ds(size_y + 8 * y, 8), 0, :] = cap

    @pl.when(leads)
    def _():
        each_peer(lambda k: slope_copy(k, chunk).wait_send())


def write_out(*refs):
    copies = [pltpu.make_async_copy(refs[i], refs[5 + i], refs[10].at[i]) for i in range(5)]
    for copy in copies:
        copy.start()
    for copy in copies:
        copy.wait()


def local(fields, spectra, permittivity, phase_start, wall_owner, cap_owner, dir_index, target, aim_mask):
    slabs, devs, xys = (lax.axis_size(a) for a in ("gz", "dev", "xy"))
    peers = slabs * devs * xys
    size_y, size_z, size_x = permittivity.shape
    assert size_z == PATCH and size_x == LANES and size_y == 4
    directions = dir_index.shape[0]
    chunks = directions // LANES
    ratio = peers // chunks
    share = directions // peers
    cap_count = size_y * size_x // PATCH
    owned = size_y + 2 * (cap_count // slabs)
    rows = 16 * size_y
    depth = size_x + 8 * size_z
    windows = 2 * STEPS
    vmem, smem = (pl.BlockSpec(memory_space=s) for s in (pltpu.VMEM, pltpu.SMEM))
    anywhere = pl.BlockSpec(memory_space=pl.ANY)
    dma = pltpu.SemaphoreType.DMA
    outs = pl.pallas_call(
        functools.partial(kernel, (slabs, devs, xys)),
        out_shape=(
            pltpu.VMEM(fields.shape, F32),
            pltpu.VMEM(spectra.shape, F32),
            pltpu.VMEM((owned, 1, LANES), F32),
            pltpu.VMEM((1, LANES), F32),
            pltpu.VMEM((size_y + cap_count, 1, LANES), F32),
        ),
        in_specs=[anywhere, anywhere, anywhere, vmem, smem, vmem, vmem, vmem, vmem],
        out_specs=(vmem,) * 5,
        scratch_shapes=[
            pltpu.VMEM((windows, 2, size_z, LANES), F32),
            pltpu.VMEM((windows, 2, size_y, 1, LANES), F32),
            pltpu.VMEM((windows, size_z, LANES), F32),
            pltpu.VMEM((windows, 2, size_z, LANES), F32),
            pltpu.VMEM((windows, 2, size_y, 1, LANES), F32),
            pltpu.VMEM((windows, size_z, LANES), F32),
            pltpu.VMEM(fields.shape, F32),
            pltpu.VMEM(spectra.shape, F32),
            pltpu.VMEM(permittivity.shape, F32),
            pltpu.VMEM((8, chunks, LANES), F32),
            pltpu.VMEM((chunks, 4, 8, LANES), F32),
            pltpu.VMEM((chunks, 2, 2 * size_y, LANES), F32),
            pltpu.VMEM((chunks, depth, 2 * LANES), BF16),
            pltpu.VMEM((chunks, depth, 2 * LANES), BF16),
            pltpu.VMEM((8 * size_y, LANES), F32),
            pltpu.VMEM((2 * rows, depth), BF16),
            pltpu.VMEM((chunks, 8, LANES), F32),
            pltpu.VMEM((peers, 8, LANES), F32),
            pltpu.VMEM((chunks, 8, LANES), F32),
            pltpu.VMEM((slabs, 8, LANES), F32),
            pltpu.VMEM((2, cap_count, LANES), F32),
            dma((windows, 3)), dma((windows, 3)),
            dma((peers,)), dma((peers,)),
            dma((peers,)), dma((chunks,)),
            dma((slabs,)), dma((slabs,)),
            dma((slabs,)), dma((2,)),
            dma((3,)),
        ],
        compiler_params=pltpu.CompilerParams(collective_id=0, has_side_effects=True),
    )(
        fields, spectra, permittivity, phase_start.reshape(1, 1), wall_owner, cap_owner,
        dir_index.reshape(chunks, LANES), target.reshape(chunks, LANES), aim_mask.reshape(chunks, LANES),
    )
    held = (fields.shape, spectra.shape, (owned, 1, LANES), (1, LANES), (size_y + cap_count, 1, LANES))
    fields_new, spectra_new, owned_rows, intensity, adjoint = pl.pallas_call(
        write_out,
        out_shape=tuple(jax.ShapeDtypeStruct(shape, F32) for shape in held),
        in_specs=[pl.BlockSpec(memory_space=pltpu.VMEM)] * 5,
        out_specs=(pl.BlockSpec(memory_space=pl.ANY),) * 5,
        scratch_shapes=[dma((5,))],
    )(*(pltpu.with_memory_space_constraint(out, pltpu.VMEM) for out in outs))
    owned_rows = owned_rows.reshape(1, 1, owned, 1, LANES).transpose(0, 1, 3, 2, 4)
    adjoint = adjoint.reshape(1, 1, size_y + cap_count, 1, LANES).transpose(0, 1, 3, 2, 4)
    intensity = intensity.reshape(LANES)
    if ratio > 1:
        me = (lax.axis_index("gz") * devs + lax.axis_index("dev")) * xys + lax.axis_index("xy")
        intensity = lax.dynamic_slice_in_dim(intensity, (me % ratio) * share, share, 0)
    return (fields_new, spectra_new, owned_rows, intensity, adjoint)


def solution(mesh):
    placed = (
        P("groups", "dev", "gz", "xy"),
        P("groups", "dev", "gz", "xy"),
        P(("groups", "dev"), "gz", "xy"),
        P("groups"),
        P("gz", None),
        P(),
        P(),
        P("groups"),
        P("groups"),
    )
    return jax.shard_map(
        local,
        mesh=mesh,
        in_specs=placed,
        out_specs=(
            P("groups", "dev", "gz", "xy"),
            P("groups", "dev", "gz", "xy"),
            P(("groups", "gz"), "dev", "xy", None, None),
            P(("groups", "gz", "dev", "xy")),
            P(("groups", "gz"), "dev", "xy", None, None),
        ),
        check_vma=False,
    )
```
